256 devices in a mesh: tm: 32 (over y_hi, z, core), head: 4 (over x), rep: 2 (over y_lo).
Axes of the slice: x: 4, y: 4 (y_hi: 2, y_lo: 2; y = y_hi * 2 + y_lo), z: 8, core: 2. Of those that a mesh axis runs over, the one named last changes fastest.
Arguments:
- queries: bfloat16 [32768, 1536], P(('tm', 'rep'), 'head'), may hold values from -8 to 8
- kv_cache: bfloat16 [32768, 2, 1536], P('tm', None, 'head'), may hold values from -8 to 8
- out_weight: bfloat16 [1536, 3072], P('head'), may hold values from -0.15625 to 0.15625
- fetch_list: int32 [64, 32], P(('tm', 'rep')), may hold values from 0 to 247, as said below
- tile_lists: int32 [256, 16], P(('tm', 'rep')), may hold values from 0 to 31, as said below
- event_offsets: int32 [256], P(('tm', 'rep')), may hold values from 0 to 7
Outputs:
- mixed: bfloat16 [32768, 3072], P(('tm', 'rep'), 'head')
The draws below stay inside these ranges and needn't reach their ends.
Inputs may be any that keep to these rules, and one draw needn't show every extreme that they name: `fetch_list`: each row names 32 distinct blocks, all with ids below (31) * 8, so none of the newest ones; one row names at most 2 blocks of one owner, and every row names exactly 2 blocks of some owner. `tile_lists`: each row names 16 distinct positions; the tiles of one device together name every position of its row of fetch_list.
All inputs are finite; a program needn't handle non-finite values.
Results may differ from the reference program's by a relative error of at most 0.013.
Values may be sent and summed in bfloat16 or wider, within the bound.
No kernel may reach another device: no remote copies, remote signals or barrier semaphores. Data moves between devices by JAX's collectives and lax.ppermute only.
A program may use at most 128 MiB of HBM per device.

```python
import math
import jax
import jax.numpy as jnp
from jax import lax

D = 3072
H = 12
DH = 128
BLK = 128
TILE = 128
CB_DEV = 8
CAP = 2
Q_DEV = 512
READERS = 64
TQ = 32768
TILES = 256
FETCH = 32
SEL = 16
CACHE_TOK = 32768
N_TM = 32
N_HEAD = 4
N_REP = 2


def draw_fetch_list(key, part):
    newest = N_TM - 1
    cand_count = N_TM * CAP

    def one_reader(reader_key, reader_index):
        key_slots, key_hot, key_noise, key_order = jax.random.split(reader_key, 4)
        slot_keys = jax.random.split(key_slots, N_TM)
        slot_perm = jax.vmap(lambda inner: jax.random.permutation(inner, CB_DEV))(slot_keys).astype(jnp.int32)
        owner_ids = jnp.arange(N_TM, dtype=jnp.int32)
        forced = (reader_index == 0) & (owner_ids == newest - 1)
        rotation = jnp.where(forced, CB_DEV - 1 - slot_perm[:, 0], 0)
        slot_pick = (slot_perm[:, :CAP] + rotation[:, None]) % CB_DEV
        candidates = (owner_ids[:, None] * CB_DEV + slot_pick).reshape(-1)
        cand_owner = jnp.repeat(owner_ids, CAP)
        drawn_hot = (newest + 1 + jax.random.randint(key_hot, (), 0, N_TM - 1)) % N_TM
        hot_owner = jnp.where(reader_index == 0, newest - 1, drawn_hot)
        noise = jax.random.randint(key_noise, (cand_count,), 0, 65536)
        ranking = noise * cand_count + jnp.arange(cand_count, dtype=jnp.int32)
        ranking = jnp.where(cand_owner == hot_owner, ranking + (1 << 28), ranking)
        ranking = jnp.where(cand_owner == newest, -1 - jnp.arange(cand_count, dtype=jnp.int32), ranking)
        unused_values, chosen_idx = lax.top_k(ranking, FETCH)
        picked = candidates[chosen_idx]
        return jax.random.permutation(key_order, picked)
    reader_keys = jax.random.split(jax.random.fold_in(key, 9), N_TM * N_REP)
    reader_ids = jnp.arange(N_TM * N_REP, dtype=jnp.int32)
    return jax.vmap(one_reader)(reader_keys, reader_ids).astype(jnp.int32)


def draw_tile_lists(key, part):
    tiles_dev = Q_DEV // TILE

    def one_reader(reader_key):
        ordering = jax.random.permutation(reader_key, FETCH).astype(jnp.int32)
        spots = (jnp.arange(tiles_dev, dtype=jnp.int32)[:, None] * SEL + jnp.arange(SEL, dtype=jnp.int32)[None, :]) % FETCH
        return ordering[spots]
    reader_keys = jax.random.split(jax.random.fold_in(key, 13), N_TM * N_REP)
    return jax.vmap(one_reader)(reader_keys).reshape(N_TM * N_REP * tiles_dev, SEL).astype(jnp.int32)


def draw_queries(key, part):
    base_draw = jax.random.truncated_normal(jax.random.fold_in(key, 31), -3.2, 3.2, (TQ, H * DH)) * 2.5
    return base_draw.astype(jnp.bfloat16)


def draw_kv_cache(key, part):
    base_draw = jax.random.truncated_normal(jax.random.fold_in(key, 41), -6.0, 6.0, (CACHE_TOK, 2, H * DH))
    return base_draw.astype(jnp.bfloat16)


def with_ends(entries, stream_key, least, top_value):
    shape = entries.shape
    place = [jax.random.randint(jax.random.fold_in(stream_key, axis), (), 0, shape[axis]) for axis in range(len(shape))]
    entries = entries.at[tuple(place)].set(least)
    longest = shape.index(max(shape))
    place[longest] = (place[longest] + 1) % shape[longest]
    return entries.at[tuple(place)].set(top_value)


def level_of(stream_key, extent, shards, low, largest):
    def one(axis_at, parts):
        draws = jax.random.uniform(jax.random.fold_in(jax.random.fold_in(stream_key, 6), axis_at), (parts,), jnp.float32, low / len(shards), largest / len(shards))
        return jnp.repeat(jnp.exp(draws), extent[axis_at] // parts).reshape((-1,) + (1,) * (len(extent) - axis_at - 1))

    factor_of = one(*shards[0])
    for cut in shards[1:]:
        factor_of = factor_of * one(*cut)
    return factor_of


def normal_values(rng, shape, spread, reach, shards=(), kind=jnp.bfloat16):
    factor_of = level_of(rng, shape, shards, -0.22, 0.18) if shards else 1.0
    values = jax.random.normal(rng, shape, jnp.float32) * spread * factor_of
    return jnp.minimum(jnp.maximum(values, -reach), reach).astype(kind)


def setup_inputs(seed: int = 0) -> dict:
    seeds = jax.random.split(jax.random.key(seed), 7)
    queries = draw_queries(jax.random.fold_in(seeds[6], 71), 0)
    kv_cache = draw_kv_cache(jax.random.fold_in(seeds[6], 71), 0)
    out_weight = normal_values(seeds[2], (H * DH, D), (H * DH) ** -0.5, 0.15625, ((0, 4),))
    fetch_list = draw_fetch_list(jax.random.fold_in(seeds[6], 71), 0)
    tile_lists = draw_tile_lists(jax.random.fold_in(seeds[6], 71), 0)
    event_offsets = with_ends(jax.random.randint(seeds[5], (TILES,), 0, CB_DEV), jax.random.fold_in(seeds[5], 1), 0, CB_DEV - 1).astype(jnp.int32)
    return {"queries": queries, "kv_cache": kv_cache, "out_weight": out_weight, "fetch_list": fetch_list, "tile_lists": tile_lists, "event_offsets": event_offsets}


def reference(queries, kv_cache, out_weight, fetch_list, tile_lists, event_offsets):
    slab_rows = CB_DEV * BLK
    score_scale = 1.0 / math.sqrt(DH)
    start_row = (N_TM - 1) * slab_rows
    panel_rows = lax.dynamic_slice_in_dim(kv_cache, start_row, slab_rows, 0)
    block_table = kv_cache.reshape(N_TM * CB_DEV, BLK, 2, H * DH)
    tiles_dev = Q_DEV // TILE
    query_tiles = queries.reshape(TILES, TILE, H, DH)
    positions = jnp.arange(slab_rows, dtype=jnp.int32)
    lit_far = jnp.ones((SEL * BLK,), dtype=bool)

    def one_tile(tile_index):
        reader = tile_index // tiles_dev
        blocks_used = fetch_list[reader][tile_lists[tile_index]]
        gathered = block_table[blocks_used].reshape(SEL * BLK, 2, H * DH)
        all_rows = jnp.concatenate([gathered, panel_rows], axis=0)
        visible = jnp.concatenate([lit_far, positions < (CB_DEV - event_offsets[tile_index]) * BLK])
        key_rows = all_rows[:, 0].reshape(-1, H, DH).astype(jnp.float32)
        value_rows = all_rows[:, 1].reshape(-1, H, DH).astype(jnp.float32)
        query_rows = query_tiles[tile_index].astype(jnp.float32)
        scores = jnp.einsum('qhd,khd->hqk', query_rows, key_rows) * score_scale
        scores = jnp.where(visible[None, None, :], scores, -1e+30)
        row_max = lax.optimization_barrier(jnp.max(scores, axis=-1, keepdims=True))
        weights = jnp.exp(scores - row_max)
        denom_sum = lax.optimization_barrier(jnp.sum(weights, axis=-1))
        rounded = lax.optimization_barrier(weights.astype(jnp.bfloat16)).astype(jnp.float32)
        blended = jnp.einsum('hqk,khd->qhd', rounded, value_rows)
        blended = blended / jnp.transpose(denom_sum)[:, :, None]
        return blended.astype(jnp.bfloat16).reshape(TILE, H * DH)
    attended = lax.map(one_tile, jnp.arange(TILES, dtype=jnp.int32)).reshape(READERS, Q_DEV, H * DH)
    group_width = H * DH // N_HEAD

    def project(rows):
        accum = jnp.zeros((Q_DEV, D), dtype=jnp.float32)
        for shard in range(N_HEAD):
            partial_value = jnp.dot(rows[:, shard * group_width:(shard + 1) * group_width], out_weight[shard * group_width:(shard + 1) * group_width], preferred_element_type=jnp.float32)
            rounded_part = lax.optimization_barrier(partial_value.astype(jnp.bfloat16))
            accum = accum + rounded_part.astype(jnp.float32)
        return accum.astype(jnp.bfloat16)
    return lax.map(project, attended).reshape(TQ, D)
```

```python
import math

import jax
import jax.numpy as jnp
from jax import lax
from jax.experimental import pallas as pl
from jax.experimental.pallas import tpu as pltpu
from jax.sharding import Mesh, PartitionSpec as P

DH = 128
TILE = 128
BLK = 128
CB_DEV = 8
SEL = 16
HALF = CB_DEV // 2
GROUP = 4
NEG = -1e30
COLUMN = ("yh", "yl")
N_COL = 4
N_X = 4
LSE_ROWS = 16


def shift(n, by):
    return [(i, (i + by) % n) for i in range(n)]


def split3(x):
    a = x.astype(jnp.bfloat16)
    rest = x - a.astype(jnp.float32)
    b = rest.astype(jnp.bfloat16)
    c = (rest - b.astype(jnp.float32)).astype(jnp.bfloat16)
    return a, b, c


def attend_kernel(counts, lists, q0, q1, q2, q3, kv, out, acc, ml):
    heads = kv.shape[1]
    scale = 1.0 / math.sqrt(DH)
    qs = (q0, q1, q2, q3)
    for r in range(4):
        q_ref = qs[r]

        @pl.loop(0, 4)
        def _(t, r=r, q_ref=q_ref):
            tile = r * 4 + t
            n = counts[tile]
            acc[...] = jnp.zeros_like(acc)
            ml[...] = jnp.full_like(ml, NEG)
            ml[8:16, :] = jnp.zeros((8, TILE), jnp.float32)
            row = pl.multiple_of(t * TILE, TILE)

            @pl.loop(0, (n + GROUP - 1) // GROUP)
            def _(g):
                base = g * GROUP
                blocks = [lists[tile, base + k] for k in range(GROUP)]
                for h in range(heads):
                    q = q_ref[pl.ds(row, TILE), h * DH : (h + 1) * DH]
                    scores = []
                    for k in range(GROUP):
                        s = lax.dot_general(
                            kv[blocks[k], h, 0],
                            q,
                            (((1,), (1,)), ((), ())),
                            preferred_element_type=jnp.float32,
                        )
                        if k:
                            s = jnp.where(base + k < n, s, NEG)
                        scores.append(s)
                    top = scores[0]
                    for s in scores[1:]:
                        top = jnp.maximum(top, s)
                    old = ml[h : h + 1, :]
                    new = jnp.maximum(old, jnp.max(top, axis=0, keepdims=True))
                    fade = jnp.exp((old - new) * scale)
                    total = None
                    mixed = None
                    for k in range(GROUP):
                        w = jnp.exp((scores[k] - new) * scale)
                        total = w if total is None else total + w
                        part = jnp.dot(
                            kv[blocks[k], h, 1],
                            w.astype(jnp.bfloat16),
                            preferred_element_type=jnp.float32,
                        )
                        mixed = part if mixed is None else mixed + part
                    ml[h : h + 1, :] = new
                    ml[8 + h : 9 + h, :] = ml[8 + h : 9 + h, :] * fade + jnp.sum(
                        total, axis=0, keepdims=True
                    )
                    acc[h] = acc[h] * fade + mixed

            for h in range(heads):
                l = ml[8 + h : 9 + h, :]
                some = l > 0.0
                lse = jnp.where(
                    some, ml[h : h + 1, :] * scale + jnp.log(jnp.where(some, l, 1.0)), NEG
                )
                inv = jnp.where(some, 1.0 / jnp.where(some, l, 1.0), 0.0)
                out[tile, h * DH : (h + 1) * DH, :] = (acc[h] * inv).astype(jnp.bfloat16)
                ml[h : h + 1, :] = lse
            a, b, c = split3(ml[0:8, :])
            out[tile, heads * DH : heads * DH + 8, :] = a
            out[tile, heads * DH + 8 : heads * DH + 16, :] = b
            out[tile, heads * DH + 16 : heads * DH + 24, :] = c
            out[tile, heads * DH + 24 : heads * DH + 32, :] = c


def attend(counts, lists, qs, kv):
    blocks, heads = kv.shape[:2]
    rows = heads * DH + 32
    return pl.pallas_call(
        attend_kernel,
        out_shape=jax.ShapeDtypeStruct((16, rows, TILE), jnp.bfloat16),
        in_specs=[pl.BlockSpec(memory_space=pltpu.SMEM)] * 2
        + [pl.BlockSpec(memory_space=pltpu.VMEM)] * 5,
        out_specs=pl.BlockSpec(memory_space=pltpu.VMEM),
        scratch_shapes=[
            pltpu.VMEM((heads, DH, TILE), jnp.float32),
            pltpu.VMEM((16, TILE), jnp.float32),
        ],
        compiler_params=pltpu.CompilerParams(vmem_limit_bytes=48 << 20),
        name="attend",
    )(counts, lists, *qs, kv)


def combine_kernel(p0, p1, p2, p3, out):
    parts = (p0, p1, p2, p3)
    heads = out.shape[1] // DH
    base = heads * DH
    for t in range(out.shape[0] // TILE):
        lses = []
        for p in parts:
            x = p[t, base : base + 24, :].astype(jnp.float32)
            lses.append(x[0:8] + x[8:16] + x[16:24])
        top = jnp.maximum(jnp.maximum(lses[0], lses[1]), jnp.maximum(lses[2], lses[3]))
        ws = [jnp.exp(x - top) for x in lses]
        inv = 1.0 / (ws[0] + ws[1] + ws[2] + ws[3])
        ws = [w * inv for w in ws]
        for h in range(heads):
            total = None
            for p, w in zip(parts, ws):
                x = p[t, h * DH : (h + 1) * DH, :].astype(jnp.float32) * w[h : h + 1, :]
                total = x if total is None else total + x
            out[t * TILE : (t + 1) * TILE, h * DH : (h + 1) * DH] = total.T.astype(jnp.bfloat16)


def combine(parts):
    tiles, rows, _ = parts[0].shape
    width = rows - 32
    return pl.pallas_call(
        combine_kernel,
        out_shape=jax.ShapeDtypeStruct((tiles * TILE, width), jnp.bfloat16),
        in_specs=[pl.BlockSpec(memory_space=pltpu.VMEM)] * 4,
        out_specs=pl.BlockSpec(memory_space=pltpu.VMEM),
        name="combine",
    )(*parts)


def block_lists(meta):
    yh, yl = lax.axis_index("yh"), lax.axis_index("yl")
    ids = meta[:, : 4 * SEL].reshape(-1, SEL)
    offsets = meta[:, 4 * SEL : 4 * SEL + 4].reshape(-1, 1)
    owners, slots = ids // CB_DEV, ids % CB_DEV
    n_owner = lax.axis_size("z") * lax.axis_size("core")
    here = (owners // n_owner == yh) & (slots % 2 == yl)
    local = (owners % n_owner) * HALF + slots // 2
    near = jnp.arange(HALF, dtype=jnp.int32)[None, :]
    seen = (near * 2 + yl < CB_DEV - offsets) & (yh == lax.axis_size("yh") - 1)
    near = jnp.broadcast_to((n_owner - 1) * HALF + near, seen.shape)
    here = jnp.concatenate([here, seen], axis=1)
    local = jnp.concatenate([local, near], axis=1)
    width = here.shape[1]
    order = jnp.arange(width, dtype=jnp.int32)
    place = jnp.sum(here[:, None, :] & (order[None, :] < order[:, None])[None], axis=2)
    hit = here[:, None, :] & (place[:, None, :] == order[None, :, None])
    lists = jnp.sum(jnp.where(hit, local[:, None, :], 0), axis=2)
    lists = jnp.pad(lists, ((0, 0), (0, 32 - width)))
    return jnp.sum(here, axis=1).astype(jnp.int32), lists.astype(jnp.int32)


def shards(queries, kv_cache, out_weight, fetch_list, tile_lists, event_offsets):
    yl, x = lax.axis_index("yl"), lax.axis_index("x")
    width = kv_cache.shape[2]
    heads = width // DH
    mine = kv_cache.reshape(HALF, 2, BLK, 2, heads, DH)
    mine = lax.dynamic_index_in_dim(mine, yl, axis=1, keepdims=False)
    keys = mine[:, :, 0].transpose(0, 2, 1, 3)
    values = mine[:, :, 1].transpose(0, 2, 3, 1)
    squares = jnp.stack([keys, values], axis=2)
    column = lax.all_gather(squares, ("z", "core"), axis=0, tiled=True)

    ids = jnp.take(fetch_list[0], tile_lists, axis=0)
    meta = jnp.concatenate([ids.reshape(-1), event_offsets, jnp.zeros((60,), jnp.int32)])[None]
    metas, qs = [meta], [queries]
    for r in range(1, N_COL):
        metas.append(lax.ppermute(meta, COLUMN, shift(N_COL, r)))
        qs.append(lax.ppermute(queries, COLUMN, shift(N_COL, r)))
    counts, lists = block_lists(jnp.concatenate(metas, axis=0))

    out_cols = out_weight.shape[1] // N_X
    pieces = out_weight.reshape(width, N_X, out_cols)
    weights = [lax.dynamic_index_in_dim(pieces, x, axis=1, keepdims=False)]
    for r in range(1, N_X):
        piece = lax.dynamic_index_in_dim(pieces, (x + r) % N_X, axis=1, keepdims=False)
        weights.append(lax.ppermute(piece, "x", shift(N_X, r)))
    weights = jnp.concatenate(weights, axis=0)

    partial = attend(counts, lists, qs, column)
    parts = [partial[0:4]]
    for r in range(1, N_COL):
        parts.append(lax.ppermute(partial[4 * r : 4 * r + 4], COLUMN, shift(N_COL, -r)))
    attended = combine(parts)
    rows = [attended]
    for r in range(1, N_X):
        rows.append(lax.ppermute(attended, "x", shift(N_X, r)))
    rows = jnp.concatenate(rows, axis=1)
    return jnp.dot(rows, weights, preferred_element_type=jnp.float32).astype(jnp.bfloat16)


def solution(mesh):
    fine = Mesh(mesh.devices.reshape(2, 8, 2, N_X, 2), ("yh", "z", "core", "x", "yl"))
    tm = ("yh", "z", "core")
    placed = (
        P((*tm, "yl"), "x"),
        P(tm, None, "x"),
        P("x", None),
        P((*tm, "yl"), None),
        P((*tm, "yl"), None),
        P((*tm, "yl")),
    )
    return jax.shard_map(
        shards, mesh=fine, in_specs=placed, out_specs=P((*tm, "yl"), "x"), check_vma=False
    )
```

```python
import functools
import math

import jax
import jax.numpy as jnp
from jax import lax
from jax.experimental import pallas as pl
from jax.experimental.pallas import tpu as pltpu
from jax.sharding import Mesh, PartitionSpec as P

DH = 128
TILE = 128
BLK = 128
CB_DEV = 8
SEL = 16
HALF = CB_DEV // 2
PAIR = 2
NEG = -1e30
COLUMN = ("yh", "yl")
N_COL = 4
N_X = 4
N_Z = 8
EXTRA = 16
ITEMS = 256
SPANS = ((0, 16), (16, 32), (32, 48), (48, 56), (56, 64))


def shift(n, by):
    return [(i, (i + by) % n) for i in range(n)]


def hop(x, axis, n, by, name):
    with jax.named_scope("s_" + name):
        return lax.ppermute(x, axis, shift(n, by))


def twin(x, name):
    with jax.named_scope("s_" + name):
        return lax.ppermute(x, "core", [(0, 1), (1, 0)])


def ring(x, name):
    up = [(z * 2, ((z + 1) % N_Z) * 2) for z in range(N_Z)]
    down = [(z * 2 + 1, ((z - 1) % N_Z) * 2 + 1) for z in range(N_Z)]
    with jax.named_scope("s_" + name):
        return lax.ppermute(x, ("z", "core"), up + down)


def after(x, *others):
    return lax.optimization_barrier((x, *others))[0]


def fetch_kernel(parity, kv, out, sems):
    heads = out.shape[1]
    copies = []
    for k in range(HALF):
        rows = pl.ds((2 * k + parity[0]) * BLK, BLK)
        for h in range(heads):
            copies.append(
                pltpu.make_async_copy(
                    kv.at[rows, :, pl.ds(h * DH, DH)], out.at[k, h], sems.at[k * heads + h]
                )
            )
    for copy in copies:
        copy.start()
    for copy in copies:
        copy.wait()


def squares_kernel(rows, out):
    at = lax.broadcasted_iota(jnp.int32, (BLK, 2 * BLK), 0) * 2
    col = lax.broadcasted_iota(jnp.int32, (BLK, 2 * BLK), 1)
    keys = (col == at).astype(jnp.bfloat16)
    values = (col == at + 1).astype(jnp.bfloat16)
    for k in range(out.shape[0]):
        for h in range(out.shape[1]):
            x = rows[k, h]
            out[k, h, 0] = jnp.dot(keys, x, preferred_element_type=jnp.float32).astype(jnp.bfloat16)
            out[k, h, 1] = lax.dot_general(
                x, values, (((0,), (1,)), ((), ())), preferred_element_type=jnp.float32
            ).astype(jnp.bfloat16)


def squares_of(kv_cache, parity):
    heads = kv_cache.shape[2] // DH
    vmem = pl.BlockSpec(memory_space=pltpu.VMEM)
    rows = pl.pallas_call(
        fetch_kernel,
        out_shape=jax.ShapeDtypeStruct((HALF, heads, BLK, 2, DH), jnp.bfloat16),
        in_specs=[pl.BlockSpec(memory_space=pltpu.SMEM), pl.BlockSpec(memory_space=pl.ANY)],
        out_specs=vmem,
        scratch_shapes=[pltpu.SemaphoreType.DMA((HALF * heads,))],
        name="fetch",
    )(parity.reshape(1).astype(jnp.int32), kv_cache)
    return pl.pallas_call(
        squares_kernel,
        out_shape=jax.ShapeDtypeStruct((HALF, heads, 2, BLK, DH), jnp.bfloat16),
        in_specs=[vmem],
        out_specs=vmem,
        name="squares",
    )(rows.reshape(HALF, heads, 2 * BLK, DH))


def attend_kernel(heads, n_kv, spans, first, *refs):
    ends, tiles_of, bases, counts, lists, q = refs[:6]
    kvs = refs[6 : 6 + n_kv]
    refs = refs[6 + n_kv :]
    if not first:
        acc_in, stat_in = refs[:2]
        refs = refs[2:]
    if spans:
        outs = refs[: len(spans)]
        acc, stat, kv, scores, sems = refs[len(spans) :]
    else:
        acc, stat, kv, scores, sems = refs
    scale = 1.0 / math.sqrt(DH)
    scale2 = scale * math.log2(math.e)
    n_heads = len(heads)
    n_tiles = q.shape[0]
    copies, at = [], 0
    for i, ref in enumerate(kvs):
        size = ref.shape[0]
        copies.append(pltpu.make_async_copy(ref, kv.at[pl.ds(at, size)], sems.at[i]))
        at += size
    for copy in copies:
        copy.start()

    @pl.loop(0, n_tiles)
    def _(tile):
        if first:
            acc[tile] = jnp.zeros(acc.shape[1:], jnp.float32)
            stat[tile, 0:8, :] = jnp.full((8, TILE), NEG, jnp.float32)
            stat[tile, 8:16, :] = jnp.zeros((8, TILE), jnp.float32)
        else:
            acc[tile] = acc_in[tile]
            stat[tile] = stat_in[tile]

    acc[n_tiles] = jnp.zeros(acc.shape[1:], jnp.float32)
    stat[n_tiles] = jnp.zeros(stat.shape[1:], jnp.float32)
    for copy in copies:
        copy.wait()

    def blocks_of(item):
        tile = jnp.minimum(tiles_of[item], n_tiles - 1)
        return tile, [lists[tile, bases[item] + k] for k in range(PAIR)]

    def score(item, slot):
        tile, blocks = blocks_of(item)
        for i, h in enumerate(heads):
            for k in range(PAIR):
                scores[slot, i, k] = lax.dot_general(
                    kv[blocks[k], i, 0],
                    q[tile, :, h * DH : (h + 1) * DH],
                    (((1,), (1,)), ((), ())),
                    preferred_element_type=jnp.float32,
                )

    def blend(item, slot):
        target = tiles_of[item]
        tile, blocks = blocks_of(item)
        left = counts[tile] - bases[item]
        lost = [jnp.where(k < left, 0.0, -NEG) for k in range(PAIR)]
        old, sums = stat[target, 0:8, :], stat[target, 8:16, :]
        rows, news, fades, adds, mixes = [], [], [], [], []
        for i in range(n_heads):
            tops = [
                jnp.max(scores[slot, i, k].reshape(BLK // 8, 8, TILE), axis=0) - lost[k]
                for k in range(PAIR)
            ]
            top = jnp.max(functools.reduce(jnp.maximum, tops), axis=0, keepdims=True)
            new = jnp.maximum(old[i : i + 1, :], top)
            news.append(new)
            fades.append(jnp.exp2((old[i : i + 1, :] - new) * scale2))
            weights = [
                jnp.exp2((scores[slot, i, k] - (new + lost[k])) * scale2) for k in range(PAIR)
            ]
            total = functools.reduce(jnp.add, weights).reshape(BLK // 8, 8, TILE)
            adds.append(jnp.sum(jnp.sum(total, axis=0), axis=0, keepdims=True))
            mixes.append(
                functools.reduce(
                    jnp.add,
                    [
                        jnp.dot(
                            kv[blocks[k], i, 1],
                            weights[k].astype(jnp.bfloat16),
                            preferred_element_type=jnp.float32,
                        )
                        for k in range(PAIR)
                    ],
                )
            )
        accs = [acc[target, i] * fades[i] + mixes[i] for i in range(n_heads)]
        for i in range(n_heads):
            acc[target, i] = accs[i]
            stat[target, i : i + 1, :] = news[i]
            stat[target, 8 + i : 9 + i, :] = sums[i : i + 1, :] * fades[i] + adds[i]

    total_items = ends[n_tiles - 1]

    @pl.when(total_items > 0)
    def _():
        score(0, 0)

        @pl.loop(0, (total_items + 1) // 2)
        def _(j):
            score(2 * j + 1, 1)
            blend(2 * j, 0)
            score(2 * j + 2, 0)
            blend(2 * j + 1, 1)

    for (tile0, tiles), out in zip(spans or (), outs if spans else ()):
        finish(n_heads, scale, tile0, tiles, acc, stat, out)


def finish(n_heads, scale, tile0, tiles, acc, stat, out):
    @pl.loop(0, tiles)
    def _(at):
        tile = tile0 + at
        total = stat[tile, 8:16, :]
        some = total > 0.0
        safe = jnp.where(some, total, 1.0)
        lse = jnp.where(some, stat[tile, 0:8, :] * scale + jnp.log(safe), NEG)
        inv = jnp.where(some, 1.0 / safe, 0.0)
        for i in range(n_heads):
            out[at, i * DH : (i + 1) * DH, :] = (acc[tile, i] * inv[i : i + 1, :]).astype(
                jnp.bfloat16
            )
        a = lse.astype(jnp.bfloat16).astype(jnp.float32)
        b = (lse - a).astype(jnp.bfloat16).astype(jnp.float32)
        c = lse - a - b
        stat[tile, 0:4, :] = a[0:4, :]
        stat[tile, 4:8, :] = b[0:4, :]
        stat[tile, 8:12, :] = c[0:4, :]
        stat[tile, 12:16, :] = c[0:4, :]
        out[at, n_heads * DH :, :] = stat[tile].astype(jnp.bfloat16)


def attend(heads, plan, q, kvs, state, spans=None):
    n_heads, tiles = len(heads), q.shape[0]
    first = state is None
    state = () if first else state
    vmem = pl.BlockSpec(memory_space=pltpu.VMEM)
    keep = [(tiles + 1, n_heads, DH, TILE), (tiles + 1, 16, TILE)]
    if spans:
        shapes = tuple(
            jax.ShapeDtypeStruct((n, n_heads * DH + EXTRA, TILE), jnp.bfloat16) for _, n in spans
        )
        scratch = [pltpu.VMEM(shape, jnp.float32) for shape in keep]
    else:
        shapes = tuple(jax.ShapeDtypeStruct(shape, jnp.float32) for shape in keep)
        scratch = []
    blocks = sum(x.shape[0] for x in kvs)
    return pl.pallas_call(
        functools.partial(attend_kernel, heads, len(kvs), spans, first),
        out_shape=shapes,
        in_specs=[pl.BlockSpec(memory_space=pltpu.SMEM)] * 5
        + [vmem]
        + [pl.BlockSpec(memory_space=pl.ANY)] * len(kvs)
        + [vmem] * len(state),
        out_specs=(vmem,) * len(shapes),
        scratch_shapes=[
            *scratch,
            pltpu.VMEM((blocks, n_heads, 2, BLK, DH), jnp.bfloat16),
            pltpu.VMEM((2, n_heads, PAIR, BLK, TILE), jnp.float32),
            pltpu.SemaphoreType.DMA((len(kvs),)),
        ],
        compiler_params=pltpu.CompilerParams(vmem_limit_bytes=14 << 20),
        cost_estimate=pl.CostEstimate(
            flops=blocks * tiles * n_heads * 20_000_000,
            bytes_accessed=blocks * n_heads * 65536,
            transcendentals=0,
        ),
        name="attend",
    )(*plan, q, *kvs, *state)


def blend_parts(parts, tile, heads):
    base = heads * DH
    lses = []
    for p in parts:
        x = p[tile, base : base + EXTRA, :].astype(jnp.float32)
        lses.append(x[0:4] + x[4:8] + x[8:12])
    top = functools.reduce(jnp.maximum, lses)
    ws = [jnp.exp(x - top) for x in lses]
    total = functools.reduce(jnp.add, ws)
    inv = 1.0 / total
    ws = [w * inv for w in ws]
    sums = []
    for h in range(heads):
        xs = [p[tile, h * DH : (h + 1) * DH, :].astype(jnp.float32) for p in parts]
        sums.append(functools.reduce(jnp.add, [x * w[h : h + 1, :] for x, w in zip(xs, ws)]))
    return sums, top + jnp.log(total)


def merge_kernel(a0, a1, b0, b1, out0, out1, stat):
    heads = (out0.shape[1] - EXTRA) // DH
    for parts, out in (((a0, a1), out0), ((b0, b1), out1)):
        for tile in range(out.shape[0]):
            sums, lse = blend_parts(parts, tile, heads)
            for h in range(heads):
                out[tile, h * DH : (h + 1) * DH, :] = sums[h].astype(jnp.bfloat16)
            a = lse.astype(jnp.bfloat16).astype(jnp.float32)
            b = (lse - a).astype(jnp.bfloat16).astype(jnp.float32)
            c = lse - a - b
            stat[0:4, :] = a
            stat[4:8, :] = b
            stat[8:12, :] = c
            stat[12:16, :] = c
            out[tile, heads * DH :, :] = stat[...].astype(jnp.bfloat16)


def merge(a0, a1, b0, b1):
    vmem = pl.BlockSpec(memory_space=pltpu.VMEM)
    return pl.pallas_call(
        merge_kernel,
        out_shape=(jax.ShapeDtypeStruct(a0.shape, a0.dtype),) * 2,
        in_specs=[vmem] * 4,
        out_specs=(vmem, vmem),
        scratch_shapes=[pltpu.VMEM((EXTRA, TILE), jnp.float32)],
        compiler_params=pltpu.CompilerParams(vmem_limit_bytes=8 << 20),
        name="merge",
    )(a0, a1, b0, b1)


def combine_kernel(own, p0, p1, out):
    heads = out.shape[1] // DH
    for tile in range(own.shape[0]):
        sums, _ = blend_parts((own, p0, p1), tile, heads)
        rows = slice(tile * TILE, (tile + 1) * TILE)
        for h in range(heads):
            out[rows, h * DH : (h + 1) * DH] = sums[h].T.astype(jnp.bfloat16)


def combine(own, p0, p1):
    tiles, rows, _ = own.shape
    vmem = pl.BlockSpec(memory_space=pltpu.VMEM)
    return pl.pallas_call(
        combine_kernel,
        out_shape=jax.ShapeDtypeStruct((tiles * TILE, rows - EXTRA), jnp.bfloat16),
        in_specs=[vmem] * 3,
        out_specs=vmem,
        compiler_params=pltpu.CompilerParams(vmem_limit_bytes=8 << 20),
        name="combine",
    )(own, p0, p1)


def project_kernel(n, more, *refs):
    out = refs[-1]
    half = out.shape[0] // 2
    step = 256
    for k in range(2):
        rows = slice(k * half, (k + 1) * half)
        for c in range(0, out.shape[1], step):
            cols = slice(c, c + step)
            parts = [
                jnp.dot(
                    refs[2 * i + k][...],
                    refs[2 * n + i][:, cols],
                    preferred_element_type=jnp.float32,
                )
                for i in range(n)
            ]
            if more:
                parts.append(refs[3 * n][rows, cols])
            out[rows, cols] = functools.reduce(jnp.add, parts).astype(out.dtype)


def project(pairs, weights, total=None):
    rows, cols = 2 * pairs[0][0].shape[0], weights[0].shape[1]
    more = () if total is None else (total,)
    flat = [x for pair in pairs for x in pair]
    vmem = pl.BlockSpec(memory_space=pltpu.VMEM)
    return pl.pallas_call(
        functools.partial(project_kernel, len(pairs), bool(more)),
        out_shape=jax.ShapeDtypeStruct((rows, cols), jnp.bfloat16 if more else jnp.float32),
        in_specs=[vmem] * (len(flat) + len(weights) + len(more)),
        out_specs=vmem,
        compiler_params=pltpu.CompilerParams(vmem_limit_bytes=14 << 20),
        cost_estimate=pl.CostEstimate(flops=10**9, bytes_accessed=4 << 20, transcendentals=0),
        name="project",
    )(*flat, *weights, *more)


def block_lists(meta):
    yh, yl = lax.axis_index("yh"), lax.axis_index("yl")
    z, core = lax.axis_index("z"), lax.axis_index("core")
    ids = meta[:, : 4 * SEL].reshape(-1, SEL)
    offsets = meta[:, 4 * SEL : 4 * SEL + 4].reshape(-1, 1)
    n_owner = N_Z * 2
    owners, slots = ids // CB_DEV, ids % CB_DEV
    here = (owners // n_owner == yh) & (slots % 2 == yl)
    near = jnp.arange(HALF, dtype=jnp.int32)[None, :]
    seen = (near * 2 + yl < CB_DEV - offsets) & (yh == lax.axis_size("yh") - 1)
    here = jnp.concatenate([here, seen], axis=1)
    owners = jnp.concatenate([owners % n_owner, jnp.full(seen.shape, n_owner - 1, jnp.int32)], axis=1)
    half = jnp.concatenate([slots // 2, jnp.broadcast_to(near, seen.shape)], axis=1)
    dist = (owners // 2 - z) % N_Z
    other = jnp.where(owners % 2 != core, 1, 0)
    ahead = dist < N_Z // 2
    step = jnp.where(ahead, dist, N_Z - dist)
    this_ring = ahead == (core == 1)
    mid = CB_DEV + 16 * (step - 1)
    mid = mid + jnp.where(this_ring, other * 8, HALF + (1 - other) * 8)
    place = jnp.where(dist == 0, other * HALF, jnp.where(dist == N_Z // 2, 56 + other * HALF, mid)) + half
    width = here.shape[1]
    order = jnp.arange(width, dtype=jnp.int32)
    lo = jnp.array([a for a, _ in SPANS], jnp.int32)[:, None, None]
    hi = jnp.array([b for _, b in SPANS], jnp.int32)[:, None, None]
    here = here[None] & (place[None] >= lo) & (place[None] < hi)
    place = place[None] - lo
    rank = jnp.sum(here[..., None, :] & (order[None, :] < order[:, None]), axis=-1)
    hit = here[..., None, :] & (rank[..., None, :] == order[:, None])
    lists = jnp.sum(jnp.where(hit, place[..., None, :], 0), axis=-1)
    lists = jnp.pad(lists, ((0, 0), (0, 0), (0, 24 - width)))
    counts = jnp.sum(here, axis=-1).astype(jnp.int32)
    return [work(counts[i], lists[i].astype(jnp.int32)) for i in range(len(SPANS))]


def work(counts, lists):
    tiles = counts.shape[0]
    pairs = (counts + PAIR - 1) // PAIR
    order = jnp.arange(tiles, dtype=jnp.int32)
    ends = jnp.sum(jnp.where(order[None, :] <= order[:, None], pairs[None, :], 0), axis=1)
    items = jnp.arange(ITEMS, dtype=jnp.int32)
    past = items[None, :] >= ends[:, None]
    tile_of = jnp.sum(past, axis=0).astype(jnp.int32)
    before = jnp.sum(jnp.where(past, pairs[:, None], 0), axis=0)
    bases = jnp.where(tile_of < tiles, (items - before) * PAIR, 0)
    return ends, tile_of, bases, counts, lists


def shards(queries, kv_cache, out_weight, fetch_list, tile_lists, event_offsets):
    yl, x = lax.axis_index("yl"), lax.axis_index("x")
    width = kv_cache.shape[2]
    mine = squares_of(kv_cache, yl)

    q_back = hop(queries, COLUMN, N_COL, 1, "q_back")
    q_next = hop(queries, COLUMN, N_COL, -1, "q_next")

    heads = (0, 1, 2)
    tw = twin(mine, "tw")
    a1 = ring(after(mine, tw), "a1")
    b1 = ring(tw, "b1")
    out_cols = out_weight.shape[1] // N_X
    out_weight = after(out_weight, tw)
    pieces = jnp.stack([out_weight[:, r * out_cols : (r + 1) * out_cols] for r in range(N_X)])
    by_peer = lax.all_to_all(pieces, "x", split_axis=0, concat_axis=0, tiled=True)
    weights = [
        lax.dynamic_index_in_dim(by_peer, (x - r) % N_X, axis=0, keepdims=False)
        for r in range(N_X)
    ]

    ids = jnp.take(after(fetch_list, a1)[0], tile_lists, axis=0)
    meta = jnp.concatenate([ids.reshape(-1), event_offsets, jnp.zeros((60,), jnp.int32)])[None]
    metas = [meta, *(hop(meta, COLUMN, N_COL, r, "meta") for r in range(1, N_COL))]
    plans = block_lists(jnp.concatenate(metas, axis=0))
    q_far = hop(after(q_back, a1), COLUMN, N_COL, 1, "q_far")
    q = jnp.concatenate([queries, q_back, q_far, q_next], axis=0)
    q = q.reshape(N_COL * 4, TILE, width)

    a2 = ring(after(a1, pieces), "a2")
    state = attend(heads, plans[0], q, [mine, tw, a1, twin(a1, "ta1")], None)
    b2 = ring(b1, "b2")
    a3 = ring(after(a2, state[1]), "a3")
    state = attend(heads, plans[1], q, [b1, twin(b1, "tb1"), a2, twin(a2, "ta2")], state)
    b3 = ring(b2, "b3")
    a4 = ring(after(a3, state[1]), "a4")
    state = attend(heads, plans[2], q, [b2, twin(b2, "tb2"), a3, twin(a3, "ta3")], state)
    state = attend(heads, plans[3], q, [b3, twin(b3, "tb3")], state)
    a4 = after(a4, state[1], *weights)
    ends = [a4, twin(a4, "ta4")]

    far0, far1, prv0, prv1, nxt0, nxt1, near0, near1 = attend(
        heads, plans[4], q, ends, state, tuple((t, 2) for t in (8, 10, 12, 14, 4, 6, 0, 2))
    )
    far0, far1 = hop(far0, COLUMN, N_COL, 1, "f0"), hop(far1, COLUMN, N_COL, -1, "f1")
    prv1, nxt0 = hop(prv1, COLUMN, N_COL, 1, "prv1"), hop(nxt0, COLUMN, N_COL, -1, "nxt0")
    prv0, nxt1 = merge(far0, prv0, far1, nxt1)
    prv0, nxt1 = hop(prv0, COLUMN, N_COL, 1, "prv0"), hop(nxt1, COLUMN, N_COL, -1, "nxt1")
    rows0, rows1 = combine(near0, prv0, nxt0), combine(near1, prv1, nxt1)

    left0, right1 = hop(rows0, "x", N_X, 1, "left0"), hop(rows1, "x", N_X, -1, "right1")
    left1, right0 = hop(rows1, "x", N_X, 1, "left1"), hop(rows0, "x", N_X, -1, "right0")
    far0, far1 = hop(left0, "x", N_X, 1, "l2"), hop(right1, "x", N_X, -1, "r2")
    total = project(
        [(rows0, rows1), (left0, left1), (right0, right1)], [weights[r] for r in (0, 1, 3)]
    )
    return project([(far0, far1)], [weights[2]], total)


def solution(mesh):
    fine = Mesh(mesh.devices.reshape(2, N_Z, 2, N_X, 2), ("yh", "z", "core", "x", "yl"))
    tm = ("yh", "z", "core")
    placed = (
        P((*tm, "yl"), "x"),
        P(tm, None, "x"),
        P("x", None),
        P((*tm, "yl"), None),
        P((*tm, "yl"), None),
        P((*tm, "yl")),
    )
    return jax.shard_map(
        shards, mesh=fine, in_specs=placed, out_specs=P((*tm, "yl"), "x"), check_vma=False
    )
```

```python
import functools
import math

import jax
import jax.numpy as jnp
from jax import lax
from jax.experimental import pallas as pl
from jax.experimental.pallas import tpu as pltpu
from jax.sharding import Mesh, PartitionSpec as P

DH = 128
TILE = 128
BLK = 128
CB_DEV = 8
SEL = 16
HALF = CB_DEV // 2
PAIR = 2
NEG = -1e30
COLUMN = ("yh", "yl")
N_COL = 4
N_X = 4
N_Z = 8
EXTRA = 16
ITEMS = 256
SPANS = ((0, 16), (16, 32), (32, 48), (48, 56), (56, 64))


def shift(n, by):
    return [(i, (i + by) % n) for i in range(n)]


def hop(x, axis, n, by, name):
    with jax.named_scope("s_" + name):
        return lax.ppermute(x, axis, shift(n, by))


def twin(x, name):
    with jax.named_scope("s_" + name):
        return lax.ppermute(x, "core", [(0, 1), (1, 0)])


def ring(x, name):
    up = [(z * 2, ((z + 1) % N_Z) * 2) for z in range(N_Z)]
    down = [(z * 2 + 1, ((z - 1) % N_Z) * 2 + 1) for z in range(N_Z)]
    with jax.named_scope("s_" + name):
        return lax.ppermute(x, ("z", "core"), up + down)


def after(x, *others):
    return lax.optimization_barrier((x, *others))[0]


def fetch_kernel(parity, kv, out, sems):
    heads = out.shape[1]
    copies = []
    for k in range(HALF):
        rows = pl.ds((2 * k + parity[0]) * BLK, BLK)
        for h in range(heads):
            copies.append(
                pltpu.make_async_copy(
                    kv.at[rows, :, pl.ds(h * DH, DH)], out.at[k, h], sems.at[k * heads + h]
                )
            )
    for copy in copies:
        copy.start()
    for copy in copies:
        copy.wait()


def squares_kernel(rows, out):
    at = lax.broadcasted_iota(jnp.int32, (BLK, 2 * BLK), 0) * 2
    col = lax.broadcasted_iota(jnp.int32, (BLK, 2 * BLK), 1)
    keys = (col == at).astype(jnp.bfloat16)
    values = (col == at + 1).astype(jnp.bfloat16)
    for k in range(out.shape[0]):
        for h in range(out.shape[1]):
            x = rows[k, h]
            out[k, h, 0] = jnp.dot(keys, x, preferred_element_type=jnp.float32).astype(jnp.bfloat16)
            out[k, h, 1] = lax.dot_general(
                x, values, (((0,), (1,)), ((), ())), preferred_element_type=jnp.float32
            ).astype(jnp.bfloat16)


def squares_of(kv_cache, parity):
    heads = kv_cache.shape[2] // DH
    vmem = pl.BlockSpec(memory_space=pltpu.VMEM)
    rows = pl.pallas_call(
        fetch_kernel,
        out_shape=jax.ShapeDtypeStruct((HALF, heads, BLK, 2, DH), jnp.bfloat16),
        in_specs=[pl.BlockSpec(memory_space=pltpu.SMEM), pl.BlockSpec(memory_space=pl.ANY)],
        out_specs=vmem,
        scratch_shapes=[pltpu.SemaphoreType.DMA((HALF * heads,))],
        name="fetch",
    )(parity.reshape(1).astype(jnp.int32), kv_cache)
    return pl.pallas_call(
        squares_kernel,
        out_shape=jax.ShapeDtypeStruct((HALF, heads, 2, BLK, DH), jnp.bfloat16),
        in_specs=[vmem],
        out_specs=vmem,
        name="squares",
    )(rows.reshape(HALF, heads, 2 * BLK, DH))


def attend_kernel(heads, n_kv, spans, first, *refs):
    ends, tiles_of, bases, counts, lists, q = refs[:6]
    kvs = refs[6 : 6 + n_kv]
    refs = refs[6 + n_kv :]
    if not first:
        acc_in, stat_in = refs[:2]
        refs = refs[2:]
    if spans:
        outs = refs[: len(spans)]
        acc, stat, kv, scores, sems = refs[len(spans) :]
    else:
        acc, stat, kv, scores, sems = refs
    scale = 1.0 / math.sqrt(DH)
    scale2 = scale * math.log2(math.e)
    n_heads = len(heads)
    n_tiles = q.shape[0]
    copies, at = [], 0
    for i, ref in enumerate(kvs):
        size = ref.shape[0]
        copies.append(pltpu.make_async_copy(ref, kv.at[pl.ds(at, size)], sems.at[i]))
        at += size
    for copy in copies:
        copy.start()

    @pl.loop(0, n_tiles)
    def _(tile):
        if first:
            acc[tile] = jnp.zeros(acc.shape[1:], jnp.float32)
            stat[tile, 0:8, :] = jnp.full((8, TILE), NEG, jnp.float32)
            stat[tile, 8:16, :] = jnp.zeros((8, TILE), jnp.float32)
        else:
            acc[tile] = acc_in[tile]
            stat[tile] = stat_in[tile]

    acc[n_tiles] = jnp.zeros(acc.shape[1:], jnp.float32)
    stat[n_tiles] = jnp.zeros(stat.shape[1:], jnp.float32)
    for copy in copies:
        copy.wait()

    def blocks_of(item):
        tile = jnp.minimum(tiles_of[item], n_tiles - 1)
        return tile, [lists[tile, bases[item] + k] for k in range(PAIR)]

    def score(item, slot):
        tile, blocks = blocks_of(item)
        for i, h in enumerate(heads):
            scores[slot, i] = lax.dot_general(
                jnp.concatenate([kv[block, i, 0] for block in blocks], axis=0),
                q[tile, :, h * DH : (h + 1) * DH],
                (((1,), (1,)), ((), ())),
                preferred_element_type=jnp.float32,
            )

    def blend(item, slot):
        target = tiles_of[item]
        tile, blocks = blocks_of(item)
        left = counts[tile] - bases[item]
        lost = [jnp.where(k < left, 0.0, -NEG) for k in range(PAIR)]
        old, sums = stat[target, 0:8, :], stat[target, 8:16, :]
        news, fades, adds, mixes = [], [], [], []
        for i in range(n_heads):
            parts = [scores[slot, i, k * BLK : (k + 1) * BLK] for k in range(PAIR)]
            tops = [
                jnp.max(s.reshape(BLK // 8, 8, TILE), axis=0) - gone for s, gone in zip(parts, lost)
            ]
            top = jnp.max(functools.reduce(jnp.maximum, tops), axis=0, keepdims=True)
            new = jnp.maximum(old[i : i + 1, :], top)
            news.append(new)
            fades.append(jnp.exp2((old[i : i + 1, :] - new) * scale2))
            weights = [jnp.exp2((s - (new + gone)) * scale2) for s, gone in zip(parts, lost)]
            total = functools.reduce(jnp.add, weights).reshape(BLK // 8, 8, TILE)
            adds.append(jnp.sum(jnp.sum(total, axis=0), axis=0, keepdims=True))
            mixes.append(
                jnp.dot(
                    jnp.concatenate([kv[block, i, 1] for block in blocks], axis=1),
                    jnp.concatenate([w.astype(jnp.bfloat16) for w in weights], axis=0),
                    preferred_element_type=jnp.float32,
                )
            )
        accs = [acc[target, i] * fades[i] + mixes[i] for i in range(n_heads)]
        for i in range(n_heads):
            acc[target, i] = accs[i]
            stat[target, i : i + 1, :] = news[i]
            stat[target, 8 + i : 9 + i, :] = sums[i : i + 1, :] * fades[i] + adds[i]

    total_items = ends[n_tiles - 1]

    @pl.when(total_items > 0)
    def _():
        score(0, 0)

        @pl.loop(0, (total_items + 1) // 2)
        def _(j):
            score(2 * j + 1, 1)
            blend(2 * j, 0)
            score(2 * j + 2, 0)
            blend(2 * j + 1, 1)

    for (tile0, tiles), out in zip(spans or (), outs if spans else ()):
        finish(n_heads, scale, tile0, tiles, acc, stat, out)


def finish(n_heads, scale, tile0, tiles, acc, stat, out):
    @pl.loop(0, tiles)
    def _(at):
        tile = tile0 + at
        total = stat[tile, 8:16, :]
        some = total > 0.0
        safe = jnp.where(some, total, 1.0)
        lse = jnp.where(some, stat[tile, 0:8, :] * scale + jnp.log(safe), NEG)
        inv = jnp.where(some, 1.0 / safe, 0.0)
        for i in range(n_heads):
            out[at, i * DH : (i + 1) * DH, :] = (acc[tile, i] * inv[i : i + 1, :]).astype(
                jnp.bfloat16
            )
        a = lse.astype(jnp.bfloat16).astype(jnp.float32)
        b = (lse - a).astype(jnp.bfloat16).astype(jnp.float32)
        c = lse - a - b
        stat[tile, 0:4, :] = a[0:4, :]
        stat[tile, 4:8, :] = b[0:4, :]
        stat[tile, 8:12, :] = c[0:4, :]
        stat[tile, 12:16, :] = c[0:4, :]
        out[at, n_heads * DH :, :] = stat[tile].astype(jnp.bfloat16)


def attend(heads, plan, q, kvs, state, spans=None):
    n_heads, tiles = len(heads), q.shape[0]
    first = state is None
    state = () if first else state
    vmem = pl.BlockSpec(memory_space=pltpu.VMEM)
    keep = [(tiles + 1, n_heads, DH, TILE), (tiles + 1, 16, TILE)]
    if spans:
        shapes = tuple(
            jax.ShapeDtypeStruct((n, n_heads * DH + EXTRA, TILE), jnp.bfloat16) for _, n in spans
        )
        scratch = [pltpu.VMEM(shape, jnp.float32) for shape in keep]
    else:
        shapes = tuple(jax.ShapeDtypeStruct(shape, jnp.float32) for shape in keep)
        scratch = []
    blocks = sum(x.shape[0] for x in kvs)
    return pl.pallas_call(
        functools.partial(attend_kernel, heads, len(kvs), spans, first),
        out_shape=shapes,
        in_specs=[pl.BlockSpec(memory_space=pltpu.SMEM)] * 5
        + [vmem]
        + [pl.BlockSpec(memory_space=pl.ANY)] * len(kvs)
        + [vmem] * len(state),
        out_specs=(vmem,) * len(shapes),
        scratch_shapes=[
            *scratch,
            pltpu.VMEM((blocks, n_heads, 2, BLK, DH), jnp.bfloat16),
            pltpu.VMEM((2, n_heads, PAIR * BLK, TILE), jnp.float32),
            pltpu.SemaphoreType.DMA((len(kvs),)),
        ],
        compiler_params=pltpu.CompilerParams(vmem_limit_bytes=14 << 20),
        cost_estimate=pl.CostEstimate(
            flops=blocks * tiles * n_heads * 20_000_000,
            bytes_accessed=blocks * n_heads * 65536,
            transcendentals=0,
        ),
        name="attend",
    )(*plan, q, *kvs, *state)


def blend_parts(parts, tile, heads):
    base = heads * DH
    lses = []
    for p in parts:
        x = p[tile, base : base + EXTRA, :].astype(jnp.float32)
        lses.append(x[0:4] + x[4:8] + x[8:12])
    top = functools.reduce(jnp.maximum, lses)
    ws = [jnp.exp(x - top) for x in lses]
    total = functools.reduce(jnp.add, ws)
    inv = 1.0 / total
    ws = [w * inv for w in ws]
    sums = []
    for h in range(heads):
        xs = [p[tile, h * DH : (h + 1) * DH, :].astype(jnp.float32) for p in parts]
        sums.append(functools.reduce(jnp.add, [x * w[h : h + 1, :] for x, w in zip(xs, ws)]))
    return sums, top + jnp.log(total)


def merge_kernel(a0, a1, b0, b1, out0, out1, stat):
    heads = (out0.shape[1] - EXTRA) // DH
    for parts, out in (((a0, a1), out0), ((b0, b1), out1)):
        for tile in range(out.shape[0]):
            sums, lse = blend_parts(parts, tile, heads)
            for h in range(heads):
                out[tile, h * DH : (h + 1) * DH, :] = sums[h].astype(jnp.bfloat16)
            a = lse.astype(jnp.bfloat16).astype(jnp.float32)
            b = (lse - a).astype(jnp.bfloat16).astype(jnp.float32)
            c = lse - a - b
            stat[0:4, :] = a
            stat[4:8, :] = b
            stat[8:12, :] = c
            stat[12:16, :] = c
            out[tile, heads * DH :, :] = stat[...].astype(jnp.bfloat16)


def merge(a0, a1, b0, b1):
    vmem = pl.BlockSpec(memory_space=pltpu.VMEM)
    return pl.pallas_call(
        merge_kernel,
        out_shape=(jax.ShapeDtypeStruct(a0.shape, a0.dtype),) * 2,
        in_specs=[vmem] * 4,
        out_specs=(vmem, vmem),
        scratch_shapes=[pltpu.VMEM((EXTRA, TILE), jnp.float32)],
        compiler_params=pltpu.CompilerParams(vmem_limit_bytes=8 << 20),
        name="merge",
    )(a0, a1, b0, b1)


def combine_kernel(own, p0, p1, out):
    heads = out.shape[1] // DH
    for tile in range(own.shape[0]):
        sums, _ = blend_parts((own, p0, p1), tile, heads)
        rows = slice(tile * TILE, (tile + 1) * TILE)
        for h in range(heads):
            out[rows, h * DH : (h + 1) * DH] = sums[h].T.astype(jnp.bfloat16)


def combine(own, p0, p1):
    tiles, rows, _ = own.shape
    vmem = pl.BlockSpec(memory_space=pltpu.VMEM)
    return pl.pallas_call(
        combine_kernel,
        out_shape=jax.ShapeDtypeStruct((tiles * TILE, rows - EXTRA), jnp.bfloat16),
        in_specs=[vmem] * 3,
        out_specs=vmem,
        compiler_params=pltpu.CompilerParams(vmem_limit_bytes=8 << 20),
        name="combine",
    )(own, p0, p1)


def project_kernel(n, more, *refs):
    out = refs[-1]
    half = out.shape[0] // 2
    step = 256
    for k in range(2):
        rows = slice(k * half, (k + 1) * half)
        for c in range(0, out.shape[1], step):
            cols = slice(c, c + step)
            parts = [
                jnp.dot(
                    refs[2 * i + k][...],
                    refs[2 * n + i][:, cols],
                    preferred_element_type=jnp.float32,
                )
                for i in range(n)
            ]
            if more:
                parts.append(refs[3 * n][rows, cols])
            out[rows, cols] = functools.reduce(jnp.add, parts).astype(out.dtype)


def project(pairs, weights, total=None):
    rows, cols = 2 * pairs[0][0].shape[0], weights[0].shape[1]
    more = () if total is None else (total,)
    flat = [x for pair in pairs for x in pair]
    vmem = pl.BlockSpec(memory_space=pltpu.VMEM)
    return pl.pallas_call(
        functools.partial(project_kernel, len(pairs), bool(more)),
        out_shape=jax.ShapeDtypeStruct((rows, cols), jnp.bfloat16 if more else jnp.float32),
        in_specs=[vmem] * (len(flat) + len(weights) + len(more)),
        out_specs=vmem,
        compiler_params=pltpu.CompilerParams(vmem_limit_bytes=14 << 20),
        cost_estimate=pl.CostEstimate(flops=10**9, bytes_accessed=4 << 20, transcendentals=0),
        name="project",
    )(*flat, *weights, *more)


def block_lists(meta):
    yh, yl = lax.axis_index("yh"), lax.axis_index("yl")
    z, core = lax.axis_index("z"), lax.axis_index("core")
    ids = meta[:, : 4 * SEL].reshape(-1, SEL)
    offsets = meta[:, 4 * SEL : 4 * SEL + 4].reshape(-1, 1)
    n_owner = N_Z * 2
    owners, slots = ids // CB_DEV, ids % CB_DEV
    here = (owners // n_owner == yh) & (slots % 2 == yl)
    near = jnp.arange(HALF, dtype=jnp.int32)[None, :]
    seen = (near * 2 + yl < CB_DEV - offsets) & (yh == lax.axis_size("yh") - 1)
    here = jnp.concatenate([here, seen], axis=1)
    owners = jnp.concatenate([owners % n_owner, jnp.full(seen.shape, n_owner - 1, jnp.int32)], axis=1)
    half = jnp.concatenate([slots // 2, jnp.broadcast_to(near, seen.shape)], axis=1)
    dist = (owners // 2 - z) % N_Z
    other = jnp.where(owners % 2 != core, 1, 0)
    ahead = dist < N_Z // 2
    step = jnp.where(ahead, dist, N_Z - dist)
    this_ring = ahead == (core == 1)
    mid = CB_DEV + 16 * (step - 1)
    mid = mid + jnp.where(this_ring, other * 8, HALF + (1 - other) * 8)
    place = jnp.where(dist == 0, other * HALF, jnp.where(dist == N_Z // 2, 56 + other * HALF, mid)) + half
    width = here.shape[1]
    order = jnp.arange(width, dtype=jnp.int32)
    lo = jnp.array([a for a, _ in SPANS], jnp.int32)[:, None, None]
    hi = jnp.array([b for _, b in SPANS], jnp.int32)[:, None, None]
    here = here[None] & (place[None] >= lo) & (place[None] < hi)
    place = place[None] - lo
    rank = jnp.sum(here[..., None, :] & (order[None, :] < order[:, None]), axis=-1)
    hit = here[..., None, :] & (rank[..., None, :] == order[:, None])
    lists = jnp.sum(jnp.where(hit, place[..., None, :], 0), axis=-1)
    lists = jnp.pad(lists, ((0, 0), (0, 0), (0, 24 - width)))
    counts = jnp.sum(here, axis=-1).astype(jnp.int32)
    return [work(counts[i], lists[i].astype(jnp.int32)) for i in range(len(SPANS))]


def work(counts, lists):
    tiles = counts.shape[0]
    pairs = (counts + PAIR - 1) // PAIR
    order = jnp.arange(tiles, dtype=jnp.int32)
    ends = jnp.sum(jnp.where(order[None, :] <= order[:, None], pairs[None, :], 0), axis=1)
    items = jnp.arange(ITEMS, dtype=jnp.int32)
    past = items[None, :] >= ends[:, None]
    tile_of = jnp.sum(past, axis=0).astype(jnp.int32)
    before = jnp.sum(jnp.where(past, pairs[:, None], 0), axis=0)
    bases = jnp.where(tile_of < tiles, (items - before) * PAIR, 0)
    return ends, tile_of, bases, counts, lists


def shards(queries, kv_cache, out_weight, fetch_list, tile_lists, event_offsets):
    yl, x = lax.axis_index("yl"), lax.axis_index("x")
    width = kv_cache.shape[2]
    mine = squares_of(kv_cache, yl)

    q_back = hop(queries, COLUMN, N_COL, 1, "q_back")
    q_next = hop(queries, COLUMN, N_COL, -1, "q_next")

    heads = (0, 1, 2)
    tw = twin(mine, "tw")
    a1 = ring(after(mine, tw), "a1")
    b1 = ring(tw, "b1")
    out_cols = out_weight.shape[1] // N_X
    out_weight = after(out_weight, tw)
    pieces = jnp.stack([out_weight[:, r * out_cols : (r + 1) * out_cols] for r in range(N_X)])
    by_peer = lax.all_to_all(pieces, "x", split_axis=0, concat_axis=0, tiled=True)
    weights = [
        lax.dynamic_index_in_dim(by_peer, (x - r) % N_X, axis=0, keepdims=False)
        for r in range(N_X)
    ]

    ids = jnp.take(after(fetch_list, pieces)[0], tile_lists, axis=0)
    meta = jnp.concatenate([ids.reshape(-1), event_offsets, jnp.zeros((60,), jnp.int32)])[None]
    metas = [meta, *(hop(meta, COLUMN, N_COL, r, "meta") for r in range(1, N_COL))]
    plans = block_lists(after(jnp.concatenate(metas, axis=0), a1))
    q_far = hop(after(q_back, a1), COLUMN, N_COL, 1, "q_far")
    q = jnp.concatenate([queries, q_back, q_far, q_next], axis=0)
    q = q.reshape(N_COL * 4, TILE, width)

    a2 = ring(after(a1, pieces), "a2")
    b2 = ring(b1, "b2")
    a3 = ring(a2, "a3")
    ta1, tb1 = twin(a1, "ta1"), twin(b1, "tb1")
    state = attend(heads, plans[0], q, [mine, tw, a1, ta1], None)
    b3 = ring(after(b2, state[1]), "b3")
    a4 = ring(a3, "a4")
    state = attend(heads, plans[1], q, [b1, after(tb1, by_peer), a2, twin(a2, "ta2")], state)
    b3, a4 = after(b3, state[1]), after(a4, state[1])
    state = attend(heads, plans[2], q, [b2, twin(b2, "tb2"), a3, twin(a3, "ta3")], state)
    state = attend(heads, plans[3], q, [b3, twin(b3, "tb3")], state)
    ends = [after(a4, *weights), twin(a4, "ta4")]

    far0, far1, prv0, prv1, nxt0, nxt1, near0, near1 = attend(
        heads, plans[4], q, ends, state, tuple((t, 2) for t in (8, 10, 12, 14, 4, 6, 0, 2))
    )
    far0, far1 = hop(far0, COLUMN, N_COL, 1, "f0"), hop(far1, COLUMN, N_COL, -1, "f1")
    prv1, nxt0 = hop(prv1, COLUMN, N_COL, 1, "prv1"), hop(nxt0, COLUMN, N_COL, -1, "nxt0")
    prv0, nxt1 = merge(far0, prv0, far1, nxt1)
    prv0, nxt1 = hop(prv0, COLUMN, N_COL, 1, "prv0"), hop(nxt1, COLUMN, N_COL, -1, "nxt1")
    rows0, rows1 = combine(near0, prv0, nxt0), combine(near1, prv1, nxt1)

    left0, right1 = hop(rows0, "x", N_X, 1, "left0"), hop(rows1, "x", N_X, -1, "right1")
    left1, right0 = hop(rows1, "x", N_X, 1, "left1"), hop(rows0, "x", N_X, -1, "right0")
    far0, far1 = hop(left0, "x", N_X, 1, "l2"), hop(right1, "x", N_X, -1, "r2")
    total = project(
        [(rows0, rows1), (left0, left1), (right0, right1)], [weights[r] for r in (0, 1, 3)]
    )
    return project([(far0, far1)], [weights[2]], total)


def solution(mesh):
    fine = Mesh(mesh.devices.reshape(2, N_Z, 2, N_X, 2), ("yh", "z", "core", "x", "yl"))
    tm = ("yh", "z", "core")
    placed = (
        P((*tm, "yl"), "x"),
        P(tm, None, "x"),
        P("x", None),
        P((*tm, "yl"), None),
        P((*tm, "yl"), None),
        P((*tm, "yl")),
    )
    return jax.shard_map(
        shards, mesh=fine, in_specs=placed, out_specs=P((*tm, "yl"), "x"), check_vma=False
    )
```

```python
import functools
import math

import jax
import jax.numpy as jnp
from jax import lax
from jax.experimental import pallas as pl
from jax.experimental.pallas import tpu as pltpu
from jax.sharding import Mesh, PartitionSpec as P

DH = 128
TILE = 128
BLK = 128
CB_DEV = 8
SEL = 16
HALF = CB_DEV // 2
PAIR = 2
NEG = -1e30
COLUMN = ("yh", "yl")
N_COL = 4
N_X = 4
N_Z = 8
EXTRA = 16
ITEMS = 256
SPANS = ((0, 16), (16, 32), (32, 48), (48, 64))


def shift(n, by):
    return [(i, (i + by) % n) for i in range(n)]


def hop(x, axis, n, by, name):
    with jax.named_scope("s_" + name):
        return lax.ppermute(x, axis, shift(n, by))


def twin(x, name):
    with jax.named_scope("s_" + name):
        return lax.ppermute(x, "core", [(0, 1), (1, 0)])


def ring(x, name):
    up = [(z * 2, ((z + 1) % N_Z) * 2) for z in range(N_Z)]
    down = [(z * 2 + 1, ((z - 1) % N_Z) * 2 + 1) for z in range(N_Z)]
    with jax.named_scope("s_" + name):
        return lax.ppermute(x, ("z", "core"), up + down)


def after(x, *others):
    return lax.optimization_barrier((x, *others))[0]


def fetch_kernel(parity, kv, out, sems):
    heads = out.shape[1]
    copies = []
    for k in range(HALF):
        rows = pl.ds((2 * k + parity[0]) * BLK, BLK)
        for h in range(heads):
            copies.append(
                pltpu.make_async_copy(
                    kv.at[rows, :, pl.ds(h * DH, DH)], out.at[k, h], sems.at[k * heads + h]
                )
            )
    for copy in copies:
        copy.start()
    for copy in copies:
        copy.wait()


def squares_kernel(rows, out):
    at = lax.broadcasted_iota(jnp.int32, (BLK, 2 * BLK), 0) * 2
    col = lax.broadcasted_iota(jnp.int32, (BLK, 2 * BLK), 1)
    keys = (col == at).astype(jnp.bfloat16)
    values = (col == at + 1).astype(jnp.bfloat16)
    for k in range(out.shape[0]):
        for h in range(out.shape[1]):
            x = rows[k, h]
            out[k, h, 0] = jnp.dot(keys, x, preferred_element_type=jnp.float32).astype(jnp.bfloat16)
            out[k, h, 1] = lax.dot_general(
                x, values, (((0,), (1,)), ((), ())), preferred_element_type=jnp.float32
            ).astype(jnp.bfloat16)


def squares_of(kv_cache, parity):
    heads = kv_cache.shape[2] // DH
    vmem = pl.BlockSpec(memory_space=pltpu.VMEM)
    rows = pl.pallas_call(
        fetch_kernel,
        out_shape=jax.ShapeDtypeStruct((HALF, heads, BLK, 2, DH), jnp.bfloat16),
        in_specs=[pl.BlockSpec(memory_space=pltpu.SMEM), pl.BlockSpec(memory_space=pl.ANY)],
        out_specs=vmem,
        scratch_shapes=[pltpu.SemaphoreType.DMA((HALF * heads,))],
        name="fetch",
    )(parity.reshape(1).astype(jnp.int32), kv_cache)
    return pl.pallas_call(
        squares_kernel,
        out_shape=jax.ShapeDtypeStruct((HALF, heads, 2, BLK, DH), jnp.bfloat16),
        in_specs=[vmem],
        out_specs=vmem,
        name="squares",
    )(rows.reshape(HALF, heads, 2 * BLK, DH))


def attend_kernel(heads, n_kv, spans, first, *refs):
    ends, tiles_of, bases, counts, lists, q = refs[:6]
    kvs = refs[6 : 6 + n_kv]
    refs = refs[6 + n_kv :]
    if not first:
        acc_in, stat_in = refs[:2]
        refs = refs[2:]
    if spans:
        outs = refs[: len(spans)]
        acc, stat, kv, scores, sems = refs[len(spans) :]
    else:
        acc, stat, kv, scores, sems = refs
    scale = 1.0 / math.sqrt(DH)
    scale2 = scale * math.log2(math.e)
    n_heads = len(heads)
    n_tiles = q.shape[0]
    copies, at = [], 0
    for i, ref in enumerate(kvs):
        size = ref.shape[0]
        copies.append(pltpu.make_async_copy(ref, kv.at[pl.ds(at, size)], sems.at[i]))
        at += size
    for copy in copies:
        copy.start()

    @pl.loop(0, n_tiles)
    def _(tile):
        if first:
            acc[tile] = jnp.zeros(acc.shape[1:], jnp.float32)
            stat[tile, 0:8, :] = jnp.full((8, TILE), NEG, jnp.float32)
            stat[tile, 8:16, :] = jnp.zeros((8, TILE), jnp.float32)
        else:
            acc[tile] = acc_in[tile]
            stat[tile] = stat_in[tile]

    acc[n_tiles] = jnp.zeros(acc.shape[1:], jnp.float32)
    stat[n_tiles] = jnp.zeros(stat.shape[1:], jnp.float32)
    for copy in copies:
        copy.wait()

    def blocks_of(item):
        tile = jnp.minimum(tiles_of[item], n_tiles - 1)
        return tile, [lists[tile, bases[item] + k] for k in range(PAIR)]

    def score(item, slot):
        tile, blocks = blocks_of(item)
        for i, h in enumerate(heads):
            scores[slot, i] = lax.dot_general(
                jnp.concatenate([kv[block, i, 0] for block in blocks], axis=0),
                q[tile, :, h * DH : (h + 1) * DH],
                (((1,), (1,)), ((), ())),
                preferred_element_type=jnp.float32,
            )

    def blend(item, slot):
        target = tiles_of[item]
        tile, blocks = blocks_of(item)
        left = counts[tile] - bases[item]
        lost = [jnp.where(k < left, 0.0, -NEG) for k in range(PAIR)]
        old, sums = stat[target, 0:8, :], stat[target, 8:16, :]
        news, fades, adds, mixes = [], [], [], []
        for i in range(n_heads):
            parts = [scores[slot, i, k * BLK : (k + 1) * BLK] for k in range(PAIR)]
            tops = [
                jnp.max(s.reshape(BLK // 8, 8, TILE), axis=0) - gone for s, gone in zip(parts, lost)
            ]
            top = jnp.max(functools.reduce(jnp.maximum, tops), axis=0, keepdims=True)
            new = jnp.maximum(old[i : i + 1, :], top)
            news.append(new)
            fades.append(jnp.exp2((old[i : i + 1, :] - new) * scale2))
            weights = [jnp.exp2((s - (new + gone)) * scale2) for s, gone in zip(parts, lost)]
            total = functools.reduce(jnp.add, weights).reshape(BLK // 8, 8, TILE)
            adds.append(jnp.sum(jnp.sum(total, axis=0), axis=0, keepdims=True))
            mixes.append(
                jnp.dot(
                    jnp.concatenate([kv[block, i, 1] for block in blocks], axis=1),
                    jnp.concatenate([w.astype(jnp.bfloat16) for w in weights], axis=0),
                    preferred_element_type=jnp.float32,
                )
            )
        accs = [acc[target, i] * fades[i] + mixes[i] for i in range(n_heads)]
        for i in range(n_heads):
            acc[target, i] = accs[i]
            stat[target, i : i + 1, :] = news[i]
            stat[target, 8 + i : 9 + i, :] = sums[i : i + 1, :] * fades[i] + adds[i]

    total_items = ends[n_tiles - 1]

    @pl.when(total_items > 0)
    def _():
        score(0, 0)

        @pl.loop(0, (total_items + 1) // 2)
        def _(j):
            score(2 * j + 1, 1)
            blend(2 * j, 0)
            score(2 * j + 2, 0)
            blend(2 * j + 1, 1)

    for (tile0, tiles), out in zip(spans or (), outs if spans else ()):
        finish(n_heads, scale, tile0, tiles, acc, stat, out)


def finish(n_heads, scale, tile0, tiles, acc, stat, out):
    @pl.loop(0, tiles)
    def _(at):
        tile = tile0 + at
        total = stat[tile, 8:16, :]
        some = total > 0.0
        safe = jnp.where(some, total, 1.0)
        lse = jnp.where(some, stat[tile, 0:8, :] * scale + jnp.log(safe), NEG)
        inv = jnp.where(some, 1.0 / safe, 0.0)
        for i in range(n_heads):
            out[at, i * DH : (i + 1) * DH, :] = (acc[tile, i] * inv[i : i + 1, :]).astype(
                jnp.bfloat16
            )
        a = lse.astype(jnp.bfloat16).astype(jnp.float32)
        b = (lse - a).astype(jnp.bfloat16).astype(jnp.float32)
        c = lse - a - b
        stat[tile, 0:4, :] = a[0:4, :]
        stat[tile, 4:8, :] = b[0:4, :]
        stat[tile, 8:12, :] = c[0:4, :]
        stat[tile, 12:16, :] = c[0:4, :]
        out[at, n_heads * DH :, :] = stat[tile].astype(jnp.bfloat16)


def attend(heads, plan, q, kvs, state, spans=None):
    n_heads, tiles = len(heads), q.shape[0]
    first = state is None
    state = () if first else state
    vmem = pl.BlockSpec(memory_space=pltpu.VMEM)
    keep = [(tiles + 1, n_heads, DH, TILE), (tiles + 1, 16, TILE)]
    if spans:
        shapes = tuple(
            jax.ShapeDtypeStruct((n, n_heads * DH + EXTRA, TILE), jnp.bfloat16) for _, n in spans
        )
        scratch = [pltpu.VMEM(shape, jnp.float32) for shape in keep]
    else:
        shapes = tuple(jax.ShapeDtypeStruct(shape, jnp.float32) for shape in keep)
        scratch = []
    blocks = sum(x.shape[0] for x in kvs)
    return pl.pallas_call(
        functools.partial(attend_kernel, heads, len(kvs), spans, first),
        out_shape=shapes,
        in_specs=[pl.BlockSpec(memory_space=pltpu.SMEM)] * 5
        + [vmem]
        + [pl.BlockSpec(memory_space=pl.ANY)] * len(kvs)
        + [vmem] * len(state),
        out_specs=(vmem,) * len(shapes),
        scratch_shapes=[
            *scratch,
            pltpu.VMEM((blocks, n_heads, 2, BLK, DH), jnp.bfloat16),
            pltpu.VMEM((2, n_heads, PAIR * BLK, TILE), jnp.float32),
            pltpu.SemaphoreType.DMA((len(kvs),)),
        ],
        compiler_params=pltpu.CompilerParams(vmem_limit_bytes=14 << 20),
        cost_estimate=pl.CostEstimate(
            flops=blocks * tiles * n_heads * 20_000_000,
            bytes_accessed=blocks * n_heads * 65536,
            transcendentals=0,
        ),
        name="attend",
    )(*plan, q, *kvs, *state)


def blend_parts(parts, tile, heads):
    base = heads * DH
    lses = []
    for p in parts:
        x = p[tile, base : base + EXTRA, :].astype(jnp.float32)
        lses.append(x[0:4] + x[4:8] + x[8:12])
    top = functools.reduce(jnp.maximum, lses)
    ws = [jnp.exp(x - top) for x in lses]
    total = functools.reduce(jnp.add, ws)
    inv = 1.0 / total
    ws = [w * inv for w in ws]
    sums = []
    for h in range(heads):
        xs = [p[tile, h * DH : (h + 1) * DH, :].astype(jnp.float32) for p in parts]
        sums.append(functools.reduce(jnp.add, [x * w[h : h + 1, :] for x, w in zip(xs, ws)]))
    return sums, top + jnp.log(total)


def merge_kernel(a0, a1, b0, b1, out0, out1, stat):
    heads = (out0.shape[1] - EXTRA) // DH
    for parts, out in (((a0, a1), out0), ((b0, b1), out1)):
        for tile in range(out.shape[0]):
            sums, lse = blend_parts(parts, tile, heads)
            for h in range(heads):
                out[tile, h * DH : (h + 1) * DH, :] = sums[h].astype(jnp.bfloat16)
            a = lse.astype(jnp.bfloat16).astype(jnp.float32)
            b = (lse - a).astype(jnp.bfloat16).astype(jnp.float32)
            c = lse - a - b
            stat[0:4, :] = a
            stat[4:8, :] = b
            stat[8:12, :] = c
            stat[12:16, :] = c
            out[tile, heads * DH :, :] = stat[...].astype(jnp.bfloat16)


def merge(a0, a1, b0, b1):
    vmem = pl.BlockSpec(memory_space=pltpu.VMEM)
    return pl.pallas_call(
        merge_kernel,
        out_shape=(jax.ShapeDtypeStruct(a0.shape, a0.dtype),) * 2,
        in_specs=[vmem] * 4,
        out_specs=(vmem, vmem),
        scratch_shapes=[pltpu.VMEM((EXTRA, TILE), jnp.float32)],
        compiler_params=pltpu.CompilerParams(vmem_limit_bytes=8 << 20),
        name="merge",
    )(a0, a1, b0, b1)


def combine_kernel(own, p0, p1, out):
    heads = out.shape[1] // DH
    for tile in range(own.shape[0]):
        sums, _ = blend_parts((own, p0, p1), tile, heads)
        rows = slice(tile * TILE, (tile + 1) * TILE)
        for h in range(heads):
            out[rows, h * DH : (h + 1) * DH] = sums[h].T.astype(jnp.bfloat16)


def combine(own, p0, p1):
    tiles, rows, _ = own.shape
    vmem = pl.BlockSpec(memory_space=pltpu.VMEM)
    return pl.pallas_call(
        combine_kernel,
        out_shape=jax.ShapeDtypeStruct((tiles * TILE, rows - EXTRA), jnp.bfloat16),
        in_specs=[vmem] * 3,
        out_specs=vmem,
        compiler_params=pltpu.CompilerParams(vmem_limit_bytes=8 << 20),
        name="combine",
    )(own, p0, p1)


def project_kernel(n, more, *refs):
    out = refs[-1]
    half = out.shape[0] // 2
    step = 256
    for k in range(2):
        rows = slice(k * half, (k + 1) * half)
        for c in range(0, out.shape[1], step):
            cols = slice(c, c + step)
            parts = [
                jnp.dot(
                    refs[2 * i + k][...],
                    refs[2 * n + i][:, cols],
                    preferred_element_type=jnp.float32,
                )
                for i in range(n)
            ]
            if more:
                parts.append(refs[3 * n][rows, cols])
            out[rows, cols] = functools.reduce(jnp.add, parts).astype(out.dtype)


def project(pairs, weights, total=None):
    rows, cols = 2 * pairs[0][0].shape[0], weights[0].shape[1]
    more = () if total is None else (total,)
    flat = [x for pair in pairs for x in pair]
    vmem = pl.BlockSpec(memory_space=pltpu.VMEM)
    return pl.pallas_call(
        functools.partial(project_kernel, len(pairs), bool(more)),
        out_shape=jax.ShapeDtypeStruct((rows, cols), jnp.bfloat16 if more else jnp.float32),
        in_specs=[vmem] * (len(flat) + len(weights) + len(more)),
        out_specs=vmem,
        compiler_params=pltpu.CompilerParams(vmem_limit_bytes=14 << 20),
        cost_estimate=pl.CostEstimate(flops=10**9, bytes_accessed=4 << 20, transcendentals=0),
        name="project",
    )(*flat, *weights, *more)


def block_lists(meta):
    yh, yl = lax.axis_index("yh"), lax.axis_index("yl")
    z, core = lax.axis_index("z"), lax.axis_index("core")
    ids = meta[:, : 4 * SEL].reshape(-1, SEL)
    offsets = meta[:, 4 * SEL : 4 * SEL + 4].reshape(-1, 1)
    n_owner = N_Z * 2
    owners, slots = ids // CB_DEV, ids % CB_DEV
    here = (owners // n_owner == yh) & (slots % 2 == yl)
    near = jnp.arange(HALF, dtype=jnp.int32)[None, :]
    seen = (near * 2 + yl < CB_DEV - offsets) & (yh == lax.axis_size("yh") - 1)
    here = jnp.concatenate([here, seen], axis=1)
    owners = jnp.concatenate([owners % n_owner, jnp.full(seen.shape, n_owner - 1, jnp.int32)], axis=1)
    half = jnp.concatenate([slots // 2, jnp.broadcast_to(near, seen.shape)], axis=1)
    dist = (owners // 2 - z) % N_Z
    other = jnp.where(owners % 2 != core, 1, 0)
    ahead = dist < N_Z // 2
    step = jnp.where(ahead, dist, N_Z - dist)
    this_ring = ahead == (core == 1)
    mid = CB_DEV + 16 * (step - 1)
    mid = mid + jnp.where(this_ring, other * 8, HALF + (1 - other) * 8)
    place = jnp.where(dist == 0, other * HALF, jnp.where(dist == N_Z // 2, 56 + other * HALF, mid)) + half
    width = here.shape[1]
    order = jnp.arange(width, dtype=jnp.int32)
    lo = jnp.array([a for a, _ in SPANS], jnp.int32)[:, None, None]
    hi = jnp.array([b for _, b in SPANS], jnp.int32)[:, None, None]
    here = here[None] & (place[None] >= lo) & (place[None] < hi)
    place = place[None] - lo
    rank = jnp.sum(here[..., None, :] & (order[None, :] < order[:, None]), axis=-1)
    hit = here[..., None, :] & (rank[..., None, :] == order[:, None])
    lists = jnp.sum(jnp.where(hit, place[..., None, :], 0), axis=-1)
    lists = jnp.pad(lists, ((0, 0), (0, 0), (0, 24 - width)))
    counts = jnp.sum(here, axis=-1).astype(jnp.int32)
    return [work(counts[i], lists[i].astype(jnp.int32)) for i in range(len(SPANS))]


def work(counts, lists):
    tiles = counts.shape[0]
    pairs = (counts + PAIR - 1) // PAIR
    order = jnp.arange(tiles, dtype=jnp.int32)
    ends = jnp.sum(jnp.where(order[None, :] <= order[:, None], pairs[None, :], 0), axis=1)
    items = jnp.arange(ITEMS, dtype=jnp.int32)
    past = items[None, :] >= ends[:, None]
    tile_of = jnp.sum(past, axis=0).astype(jnp.int32)
    before = jnp.sum(jnp.where(past, pairs[:, None], 0), axis=0)
    bases = jnp.where(tile_of < tiles, (items - before) * PAIR, 0)
    return ends, tile_of, bases, counts, lists


def shards(queries, kv_cache, out_weight, fetch_list, tile_lists, event_offsets):
    yl, x = lax.axis_index("yl"), lax.axis_index("x")
    width = kv_cache.shape[2]
    mine = squares_of(kv_cache, yl)

    q_back = hop(queries, COLUMN, N_COL, 1, "q_back")
    q_next = hop(queries, COLUMN, N_COL, -1, "q_next")

    heads = (0, 1, 2)
    tw = twin(mine, "tw")
    a1 = ring(after(mine, tw), "a1")
    b1 = ring(tw, "b1")
    out_cols = out_weight.shape[1] // N_X
    out_weight = after(out_weight, tw)
    pieces = jnp.stack([out_weight[:, r * out_cols : (r + 1) * out_cols] for r in range(N_X)])
    by_peer = lax.all_to_all(pieces, "x", split_axis=0, concat_axis=0, tiled=True)
    weights = [
        lax.dynamic_index_in_dim(by_peer, (x - r) % N_X, axis=0, keepdims=False)
        for r in range(N_X)
    ]

    ids = jnp.take(after(fetch_list, pieces)[0], tile_lists, axis=0)
    meta = jnp.concatenate([ids.reshape(-1), event_offsets, jnp.zeros((60,), jnp.int32)])[None]
    metas = [meta, *(hop(meta, COLUMN, N_COL, r, "meta") for r in range(1, N_COL))]
    plans = block_lists(after(jnp.concatenate(metas, axis=0), a1))
    q_far = hop(after(q_back, a1), COLUMN, N_COL, 1, "q_far")
    q = jnp.concatenate([queries, q_back, q_far, q_next], axis=0)
    q = q.reshape(N_COL * 4, TILE, width)

    a2 = ring(after(a1, pieces), "a2")
    b2 = ring(b1, "b2")
    a3 = ring(a2, "a3")
    ta1, tb1 = twin(a1, "ta1"), twin(b1, "tb1")
    state = attend(heads, plans[0], q, [mine, tw, a1, ta1], None)
    b3 = ring(after(b2, state[1]), "b3")
    a4 = ring(a3, "a4")
    state = attend(heads, plans[1], q, [b1, after(tb1, by_peer), a2, twin(a2, "ta2")], state)
    b3, a4 = after(b3, state[1]), after(a4, state[1])
    state = attend(heads, plans[2], q, [b2, twin(b2, "tb2"), a3, twin(a3, "ta3")], state)
    ends = [b3, twin(b3, "tb3"), after(a4, *weights), twin(a4, "ta4")]

    far0, far1, prv0, prv1, nxt0, nxt1, near0, near1 = attend(
        heads, plans[3], q, ends, state, tuple((t, 2) for t in (8, 10, 12, 14, 4, 6, 0, 2))
    )
    far0, far1 = hop(far0, COLUMN, N_COL, 1, "f0"), hop(far1, COLUMN, N_COL, -1, "f1")
    prv1, nxt0 = hop(prv1, COLUMN, N_COL, 1, "prv1"), hop(nxt0, COLUMN, N_COL, -1, "nxt0")
    prv0, nxt1 = merge(far0, prv0, far1, nxt1)
    prv0, nxt1 = hop(prv0, COLUMN, N_COL, 1, "prv0"), hop(nxt1, COLUMN, N_COL, -1, "nxt1")
    rows0, rows1 = combine(near0, prv0, nxt0), combine(near1, prv1, nxt1)

    left0, right1 = hop(rows0, "x", N_X, 1, "left0"), hop(rows1, "x", N_X, -1, "right1")
    left1, right0 = hop(rows1, "x", N_X, 1, "left1"), hop(rows0, "x", N_X, -1, "right0")
    far0, far1 = hop(left0, "x", N_X, 1, "l2"), hop(right1, "x", N_X, -1, "r2")
    total = project(
        [(rows0, rows1), (left0, left1), (right0, right1)], [weights[r] for r in (0, 1, 3)]
    )
    return project([(far0, far1)], [weights[2]], total)


def solution(mesh):
    fine = Mesh(mesh.devices.reshape(2, N_Z, 2, N_X, 2), ("yh", "z", "core", "x", "yl"))
    tm = ("yh", "z", "core")
    placed = (
        P((*tm, "yl"), "x"),
        P(tm, None, "x"),
        P("x", None),
        P((*tm, "yl"), None),
        P((*tm, "yl"), None),
        P((*tm, "yl")),
    )
    return jax.shard_map(
        shards, mesh=fine, in_specs=placed, out_specs=P((*tm, "yl"), "x"), check_vma=False
    )
```

```python
import functools
import math

import jax
import jax.numpy as jnp
from jax import lax
from jax.experimental import pallas as pl
from jax.experimental.pallas import tpu as pltpu
from jax.sharding import Mesh, PartitionSpec as P

DH = 128
TILE = 128
BLK = 128
CB_DEV = 8
SEL = 16
HALF = CB_DEV // 2
PAIR = 2
NEG = -1e30
COLUMN = ("yh", "yl")
N_COL = 4
N_X = 4
N_Z = 8
EXTRA = 16
ITEMS = 256
SPANS = ((0, 16), (16, 32), (32, 48), (48, 64))


def shift(n, by):
    return [(i, (i + by) % n) for i in range(n)]


def hop(x, axis, n, by, name):
    with jax.named_scope("s_" + name):
        return lax.ppermute(x, axis, shift(n, by))


def twin(x, name):
    with jax.named_scope("s_" + name):
        return lax.ppermute(x, "core", [(0, 1), (1, 0)])


def ring(x, name):
    up = [(z * 2, ((z + 1) % N_Z) * 2) for z in range(N_Z)]
    down = [(z * 2 + 1, ((z - 1) % N_Z) * 2 + 1) for z in range(N_Z)]
    with jax.named_scope("s_" + name):
        return lax.ppermute(x, ("z", "core"), up + down)


def after(x, *others):
    return lax.optimization_barrier((x, *others))[0]


def fetch_kernel(parity, kv, out, sems):
    heads = out.shape[1]
    copies = []
    for k in range(HALF):
        rows = pl.ds((2 * k + parity[0]) * BLK, BLK)
        for h in range(heads):
            copies.append(
                pltpu.make_async_copy(
                    kv.at[rows, :, pl.ds(h * DH, DH)], out.at[k, h], sems.at[k * heads + h]
                )
            )
    for copy in copies:
        copy.start()
    for copy in copies:
        copy.wait()


def squares_kernel(rows, out):
    at = lax.broadcasted_iota(jnp.int32, (BLK, 2 * BLK), 0) * 2
    col = lax.broadcasted_iota(jnp.int32, (BLK, 2 * BLK), 1)
    keys = (col == at).astype(jnp.bfloat16)
    values = (col == at + 1).astype(jnp.bfloat16)
    for k in range(out.shape[0]):
        for h in range(out.shape[1]):
            x = rows[k, h]
            out[k, h, 0] = jnp.dot(keys, x, preferred_element_type=jnp.float32).astype(jnp.bfloat16)
            out[k, h, 1] = lax.dot_general(
                x, values, (((0,), (1,)), ((), ())), preferred_element_type=jnp.float32
            ).astype(jnp.bfloat16)


def squares_of(kv_cache, parity):
    heads = kv_cache.shape[2] // DH
    vmem = pl.BlockSpec(memory_space=pltpu.VMEM)
    rows = pl.pallas_call(
        fetch_kernel,
        out_shape=jax.ShapeDtypeStruct((HALF, heads, BLK, 2, DH), jnp.bfloat16),
        in_specs=[pl.BlockSpec(memory_space=pltpu.SMEM), pl.BlockSpec(memory_space=pl.ANY)],
        out_specs=vmem,
        scratch_shapes=[pltpu.SemaphoreType.DMA((HALF * heads,))],
        name="fetch",
    )(parity.reshape(1).astype(jnp.int32), kv_cache)
    return pl.pallas_call(
        squares_kernel,
        out_shape=jax.ShapeDtypeStruct((HALF, heads, 2, BLK, DH), jnp.bfloat16),
        in_specs=[vmem],
        out_specs=vmem,
        name="squares",
    )(rows.reshape(HALF, heads, 2 * BLK, DH))


def attend_kernel(heads, n_kv, spans, first, *refs):
    ends, tiles_of, bases, counts, lists, q = refs[:6]
    kvs = refs[6 : 6 + n_kv]
    refs = refs[6 + n_kv :]
    if not first:
        acc_in, stat_in = refs[:2]
        refs = refs[2:]
    if spans:
        outs = refs[: len(spans)]
        acc, stat, kv, scores, sems = refs[len(spans) :]
    else:
        acc, stat, kv, scores, sems = refs
    scale = 1.0 / math.sqrt(DH)
    scale2 = scale * math.log2(math.e)
    n_heads = len(heads)
    n_tiles = q.shape[0]
    copies, at = [], 0
    for i, ref in enumerate(kvs):
        size = ref.shape[0]
        copies.append(pltpu.make_async_copy(ref, kv.at[pl.ds(at, size)], sems.at[i]))
        at += size
    for copy in copies:
        copy.start()

    @pl.loop(0, n_tiles)
    def _(tile):
        if first:
            acc[tile] = jnp.zeros(acc.shape[1:], jnp.float32)
            stat[tile, 0:8, :] = jnp.full((8, TILE), NEG, jnp.float32)
            stat[tile, 8:16, :] = jnp.zeros((8, TILE), jnp.float32)
        else:
            acc[tile] = acc_in[tile]
            stat[tile] = stat_in[tile]

    acc[n_tiles] = jnp.zeros(acc.shape[1:], jnp.float32)
    stat[n_tiles] = jnp.zeros(stat.shape[1:], jnp.float32)
    for copy in copies:
        copy.wait()

    def blocks_of(item):
        tile = jnp.minimum(tiles_of[item], n_tiles - 1)
        return tile, [lists[tile, bases[item] + k] for k in range(PAIR)]

    def score(item, slot):
        tile, blocks = blocks_of(item)
        for i, h in enumerate(heads):
            scores[slot, i] = lax.dot_general(
                jnp.concatenate([kv[block, i, 0] for block in blocks], axis=0),
                q[tile, :, h * DH : (h + 1) * DH],
                (((1,), (1,)), ((), ())),
                preferred_element_type=jnp.float32,
            )

    def blend(item, slot):
        target = tiles_of[item]
        tile, blocks = blocks_of(item)
        left = counts[tile] - bases[item]
        lost = [jnp.where(k < left, 0.0, -NEG) for k in range(PAIR)]
        old, sums = stat[target, 0:8, :], stat[target, 8:16, :]
        news, fades, adds, mixes = [], [], [], []
        for i in range(n_heads):
            parts = [scores[slot, i, k * BLK : (k + 1) * BLK] for k in range(PAIR)]
            tops = [
                jnp.max(s.reshape(BLK // 8, 8, TILE), axis=0) - gone for s, gone in zip(parts, lost)
            ]
            top = jnp.max(functools.reduce(jnp.maximum, tops), axis=0, keepdims=True)
            new = jnp.maximum(old[i : i + 1, :], top)
            news.append(new)
            fades.append(jnp.exp2((old[i : i + 1, :] - new) * scale2))
            weights = [jnp.exp2((s - (new + gone)) * scale2) for s, gone in zip(parts, lost)]
            total = functools.reduce(jnp.add, weights).reshape(BLK // 8, 8, TILE)
            adds.append(jnp.sum(jnp.sum(total, axis=0), axis=0, keepdims=True))
            mixes.append(
                jnp.dot(
                    jnp.concatenate([kv[block, i, 1] for block in blocks], axis=1),
                    jnp.concatenate([w.astype(jnp.bfloat16) for w in weights], axis=0),
                    preferred_element_type=jnp.float32,
                )
            )
        accs = [acc[target, i] * fades[i] + mixes[i] for i in range(n_heads)]
        for i in range(n_heads):
            acc[target, i] = accs[i]
            stat[target, i : i + 1, :] = news[i]
            stat[target, 8 + i : 9 + i, :] = sums[i : i + 1, :] * fades[i] + adds[i]

    total_items = ends[n_tiles - 1]

    @pl.when(total_items > 0)
    def _():
        score(0, 0)

        @pl.loop(0, (total_items + 1) // 2)
        def _(j):
            score(2 * j + 1, 1)
            blend(2 * j, 0)
            score(2 * j + 2, 0)
            blend(2 * j + 1, 1)

    for (tile0, tiles), out in zip(spans or (), outs if spans else ()):
        finish(n_heads, scale, tile0, tiles, acc, stat, out)


def finish(n_heads, scale, tile0, tiles, acc, stat, out):
    @pl.loop(0, tiles)
    def _(at):
        tile = tile0 + at
        total = stat[tile, 8:16, :]
        some = total > 0.0
        safe = jnp.where(some, total, 1.0)
        lse = jnp.where(some, stat[tile, 0:8, :] * scale + jnp.log(safe), NEG)
        inv = jnp.where(some, 1.0 / safe, 0.0)
        for i in range(n_heads):
            out[at, i * DH : (i + 1) * DH, :] = (acc[tile, i] * inv[i : i + 1, :]).astype(
                jnp.bfloat16
            )
        a = lse.astype(jnp.bfloat16).astype(jnp.float32)
        b = (lse - a).astype(jnp.bfloat16).astype(jnp.float32)
        c = lse - a - b
        stat[tile, 0:4, :] = a[0:4, :]
        stat[tile, 4:8, :] = b[0:4, :]
        stat[tile, 8:12, :] = c[0:4, :]
        stat[tile, 12:16, :] = c[0:4, :]
        out[at, n_heads * DH :, :] = stat[tile].astype(jnp.bfloat16)


def attend(heads, plan, q, kvs, state, spans=None):
    n_heads, tiles = len(heads), q.shape[0]
    first = state is None
    state = () if first else state
    vmem = pl.BlockSpec(memory_space=pltpu.VMEM)
    keep = [(tiles + 1, n_heads, DH, TILE), (tiles + 1, 16, TILE)]
    if spans:
        shapes = tuple(
            jax.ShapeDtypeStruct((n, n_heads * DH + EXTRA, TILE), jnp.bfloat16) for _, n in spans
        )
        scratch = [pltpu.VMEM(shape, jnp.float32) for shape in keep]
    else:
        shapes = tuple(jax.ShapeDtypeStruct(shape, jnp.float32) for shape in keep)
        scratch = []
    blocks = sum(x.shape[0] for x in kvs)
    return pl.pallas_call(
        functools.partial(attend_kernel, heads, len(kvs), spans, first),
        out_shape=shapes,
        in_specs=[pl.BlockSpec(memory_space=pltpu.SMEM)] * 5
        + [vmem]
        + [pl.BlockSpec(memory_space=pl.ANY)] * len(kvs)
        + [vmem] * len(state),
        out_specs=(vmem,) * len(shapes),
        scratch_shapes=[
            *scratch,
            pltpu.VMEM((blocks, n_heads, 2, BLK, DH), jnp.bfloat16),
            pltpu.VMEM((2, n_heads, PAIR * BLK, TILE), jnp.float32),
            pltpu.SemaphoreType.DMA((len(kvs),)),
        ],
        compiler_params=pltpu.CompilerParams(vmem_limit_bytes=14 << 20),
        cost_estimate=pl.CostEstimate(
            flops=blocks * tiles * n_heads * 20_000_000,
            bytes_accessed=blocks * n_heads * 65536,
            transcendentals=0,
        ),
        name="attend",
    )(*plan, q, *kvs, *state)


def blend_parts(parts, tile, heads):
    base = heads * DH
    lses = []
    for p in parts:
        x = p[tile, base : base + EXTRA, :].astype(jnp.float32)
        lses.append(x[0:4] + x[4:8] + x[8:12])
    top = functools.reduce(jnp.maximum, lses)
    ws = [jnp.exp(x - top) for x in lses]
    total = functools.reduce(jnp.add, ws)
    inv = 1.0 / total
    ws = [w * inv for w in ws]
    sums = []
    for h in range(heads):
        xs = [p[tile, h * DH : (h + 1) * DH, :].astype(jnp.float32) for p in parts]
        sums.append(functools.reduce(jnp.add, [x * w[h : h + 1, :] for x, w in zip(xs, ws)]))
    return sums, top + jnp.log(total)


def merge_kernel(a0, a1, b0, b1, out0, out1, stat):
    heads = (out0.shape[1] - EXTRA) // DH
    for parts, out in (((a0, a1), out0), ((b0, b1), out1)):
        for tile in range(out.shape[0]):
            sums, lse = blend_parts(parts, tile, heads)
            for h in range(heads):
                out[tile, h * DH : (h + 1) * DH, :] = sums[h].astype(jnp.bfloat16)
            a = lse.astype(jnp.bfloat16).astype(jnp.float32)
            b = (lse - a).astype(jnp.bfloat16).astype(jnp.float32)
            c = lse - a - b
            stat[0:4, :] = a
            stat[4:8, :] = b
            stat[8:12, :] = c
            stat[12:16, :] = c
            out[tile, heads * DH :, :] = stat[...].astype(jnp.bfloat16)


def merge(a0, a1, b0, b1):
    vmem = pl.BlockSpec(memory_space=pltpu.VMEM)
    return pl.pallas_call(
        merge_kernel,
        out_shape=(jax.ShapeDtypeStruct(a0.shape, a0.dtype),) * 2,
        in_specs=[vmem] * 4,
        out_specs=(vmem, vmem),
        scratch_shapes=[pltpu.VMEM((EXTRA, TILE), jnp.float32)],
        compiler_params=pltpu.CompilerParams(vmem_limit_bytes=8 << 20),
        name="merge",
    )(a0, a1, b0, b1)


def combine_kernel(own, p0, p1, out):
    heads = out.shape[1] // DH
    for tile in range(own.shape[0]):
        sums, _ = blend_parts((own, p0, p1), tile, heads)
        rows = slice(tile * TILE, (tile + 1) * TILE)
        for h in range(heads):
            out[rows, h * DH : (h + 1) * DH] = sums[h].T.astype(jnp.bfloat16)


def combine(own, p0, p1):
    tiles, rows, _ = own.shape
    vmem = pl.BlockSpec(memory_space=pltpu.VMEM)
    return pl.pallas_call(
        combine_kernel,
        out_shape=jax.ShapeDtypeStruct((tiles * TILE, rows - EXTRA), jnp.bfloat16),
        in_specs=[vmem] * 3,
        out_specs=vmem,
        compiler_params=pltpu.CompilerParams(vmem_limit_bytes=8 << 20),
        name="combine",
    )(own, p0, p1)


def project_kernel(n, more, *refs):
    out = refs[-1]
    half = out.shape[0] // 2
    step = 256
    for k in range(2):
        rows = slice(k * half, (k + 1) * half)
        for c in range(0, out.shape[1], step):
            cols = slice(c, c + step)
            parts = [
                jnp.dot(
                    refs[2 * i + k][...],
                    refs[2 * n + i][:, cols],
                    preferred_element_type=jnp.float32,
                )
                for i in range(n)
            ]
            if more:
                parts.append(refs[3 * n][rows, cols])
            out[rows, cols] = functools.reduce(jnp.add, parts).astype(out.dtype)


def project(pairs, weights, total=None):
    rows, cols = 2 * pairs[0][0].shape[0], weights[0].shape[1]
    more = () if total is None else (total,)
    flat = [x for pair in pairs for x in pair]
    vmem = pl.BlockSpec(memory_space=pltpu.VMEM)
    return pl.pallas_call(
        functools.partial(project_kernel, len(pairs), bool(more)),
        out_shape=jax.ShapeDtypeStruct((rows, cols), jnp.bfloat16 if more else jnp.float32),
        in_specs=[vmem] * (len(flat) + len(weights) + len(more)),
        out_specs=vmem,
        compiler_params=pltpu.CompilerParams(vmem_limit_bytes=14 << 20),
        cost_estimate=pl.CostEstimate(flops=10**9, bytes_accessed=4 << 20, transcendentals=0),
        name="project",
    )(*flat, *weights, *more)


def block_lists(meta):
    yh, yl = lax.axis_index("yh"), lax.axis_index("yl")
    z, core = lax.axis_index("z"), lax.axis_index("core")
    ids = meta[:, : 4 * SEL].reshape(-1, SEL)
    offsets = meta[:, 4 * SEL : 4 * SEL + 4].reshape(-1, 1)
    n_owner = N_Z * 2
    owners, slots = ids // CB_DEV, ids % CB_DEV
    here = (owners // n_owner == yh) & (slots % 2 == yl)
    near = jnp.arange(HALF, dtype=jnp.int32)[None, :]
    seen = (near * 2 + yl < CB_DEV - offsets) & (yh == lax.axis_size("yh") - 1)
    here = jnp.concatenate([here, seen], axis=1)
    owners = jnp.concatenate([owners % n_owner, jnp.full(seen.shape, n_owner - 1, jnp.int32)], axis=1)
    half = jnp.concatenate([slots // 2, jnp.broadcast_to(near, seen.shape)], axis=1)
    dist = (owners // 2 - z) % N_Z
    other = jnp.where(owners % 2 != core, 1, 0)
    ahead = dist < N_Z // 2
    step = jnp.where(ahead, dist, N_Z - dist)
    this_ring = ahead == (core == 1)
    mid = CB_DEV + 16 * (step - 1)
    mid = mid + jnp.where(this_ring, other * 8, HALF + (1 - other) * 8)
    place = jnp.where(dist == 0, other * HALF, jnp.where(dist == N_Z // 2, 56 + other * HALF, mid)) + half
    width = here.shape[1]
    order = jnp.arange(width, dtype=jnp.int32)
    lo = jnp.array([a for a, _ in SPANS], jnp.int32)[:, None, None]
    hi = jnp.array([b for _, b in SPANS], jnp.int32)[:, None, None]
    here = here[None] & (place[None] >= lo) & (place[None] < hi)
    place = place[None] - lo
    rank = jnp.sum(here[..., None, :] & (order[None, :] < order[:, None]), axis=-1)
    hit = here[..., None, :] & (rank[..., None, :] == order[:, None])
    lists = jnp.sum(jnp.where(hit, place[..., None, :], 0), axis=-1)
    lists = jnp.pad(lists, ((0, 0), (0, 0), (0, 24 - width)))
    counts = jnp.sum(here, axis=-1).astype(jnp.int32)
    return [work(counts[i], lists[i].astype(jnp.int32)) for i in range(len(SPANS))]


def work(counts, lists):
    tiles = counts.shape[0]
    pairs = (counts + PAIR - 1) // PAIR
    order = jnp.arange(tiles, dtype=jnp.int32)
    ends = jnp.sum(jnp.where(order[None, :] <= order[:, None], pairs[None, :], 0), axis=1)
    items = jnp.arange(ITEMS, dtype=jnp.int32)
    past = items[None, :] >= ends[:, None]
    tile_of = jnp.sum(past, axis=0).astype(jnp.int32)
    before = jnp.sum(jnp.where(past, pairs[:, None], 0), axis=0)
    bases = jnp.where(tile_of < tiles, (items - before) * PAIR, 0)
    return ends, tile_of, bases, counts, lists


def shards(queries, kv_cache, out_weight, fetch_list, tile_lists, event_offsets):
    yl, x = lax.axis_index("yl"), lax.axis_index("x")
    width = kv_cache.shape[2]
    mine = squares_of(kv_cache, yl)

    q_back = hop(queries, COLUMN, N_COL, 1, "q_back")
    q_next = hop(queries, COLUMN, N_COL, -1, "q_next")

    heads = (0, 1, 2)
    tw = twin(mine, "tw")
    a1 = ring(after(mine, tw), "a1")
    b1 = ring(tw, "b1")
    out_cols = out_weight.shape[1] // N_X
    out_weight = after(out_weight, tw)
    pieces = jnp.stack([out_weight[:, r * out_cols : (r + 1) * out_cols] for r in range(N_X)])
    by_peer = lax.all_to_all(pieces, "x", split_axis=0, concat_axis=0, tiled=True)

    ids = jnp.take(after(fetch_list, pieces)[0], tile_lists, axis=0)
    meta = jnp.concatenate([ids.reshape(-1), event_offsets, jnp.zeros((60,), jnp.int32)])[None]
    metas = [meta, *(hop(meta, COLUMN, N_COL, r, "meta") for r in range(1, N_COL))]
    plans = block_lists(after(jnp.concatenate(metas, axis=0), a1))
    q_far = hop(after(q_back, a1), COLUMN, N_COL, 1, "q_far")
    q = jnp.concatenate([queries, q_back, q_far, q_next], axis=0)
    q = q.reshape(N_COL * 4, TILE, width)

    a2 = ring(after(a1, pieces), "a2")
    b2 = ring(b1, "b2")
    a3 = ring(a2, "a3")
    ta1, tb1 = twin(a1, "ta1"), twin(b1, "tb1")
    state = attend(heads, plans[0], q, [mine, tw, a1, ta1], None)
    b3 = ring(after(b2, state[1]), "b3")
    a4 = ring(a3, "a4")
    state = attend(heads, plans[1], q, [b1, after(tb1, by_peer), a2, twin(a2, "ta2")], state)
    b3, a4 = after(b3, state[1]), after(a4, state[1])
    state = attend(heads, plans[2], q, [b2, twin(b2, "tb2"), a3, twin(a3, "ta3")], state)
    ends = [b3, twin(b3, "tb3"), a4, twin(a4, "ta4")]

    far0, far1, prv0, prv1, nxt0, nxt1, near0, near1 = attend(
        heads, plans[3], q, ends, state, tuple((t, 2) for t in (8, 10, 12, 14, 4, 6, 0, 2))
    )
    far0, far1 = hop(far0, COLUMN, N_COL, 1, "f0"), hop(far1, COLUMN, N_COL, -1, "f1")
    prv1, nxt0 = hop(prv1, COLUMN, N_COL, 1, "prv1"), hop(nxt0, COLUMN, N_COL, -1, "nxt0")
    prv0, nxt1 = merge(far0, prv0, far1, nxt1)
    by_peer = after(by_peer, nxt1)
    weights = [
        lax.dynamic_index_in_dim(by_peer, (x - r) % N_X, axis=0, keepdims=False)
        for r in range(N_X)
    ]
    prv0, nxt1 = hop(prv0, COLUMN, N_COL, 1, "prv0"), hop(nxt1, COLUMN, N_COL, -1, "nxt1")
    rows0, rows1 = combine(near0, prv0, nxt0), combine(near1, prv1, nxt1)

    left0, right1 = hop(rows0, "x", N_X, 1, "left0"), hop(rows1, "x", N_X, -1, "right1")
    left1, right0 = hop(rows1, "x", N_X, 1, "left1"), hop(rows0, "x", N_X, -1, "right0")
    far0, far1 = hop(left0, "x", N_X, 1, "l2"), hop(right1, "x", N_X, -1, "r2")
    total = project(
        [(rows0, rows1), (left0, left1), (right0, right1)], [weights[r] for r in (0, 1, 3)]
    )
    return project([(far0, far1)], [weights[2]], total)


def solution(mesh):
    fine = Mesh(mesh.devices.reshape(2, N_Z, 2, N_X, 2), ("yh", "z", "core", "x", "yl"))
    tm = ("yh", "z", "core")
    placed = (
        P((*tm, "yl"), "x"),
        P(tm, None, "x"),
        P("x", None),
        P((*tm, "yl"), None),
        P((*tm, "yl"), None),
        P((*tm, "yl")),
    )
    return jax.shard_map(
        shards, mesh=fine, in_specs=placed, out_specs=P((*tm, "yl"), "x"), check_vma=False
    )
```
